32 devices in a mesh: dp: 2 (over x), tm: 4 (over z), space: 4 (over y, core).
Axes of the slice: x: 2, y: 2, z: 4, core: 2. Of those that a mesh axis runs over, the one named last changes fastest.
Arguments:
- latents: bfloat16 [2, 8, 8, 128, 512], P('dp', 'tm', 'space'), may hold values from -400 to 400
- owner: int32 [2, 4, 1], P('dp'), may hold values from 0 to 3; in each aligned block of 4 rows (0 to 3, 4 to 7, ..., all dimensions but the last counted through in order) at most 2 rows name the same one
- gamma: float32 [512], replicated, may hold values from 0.25 to 1.75
- beta: float32 [512], replicated, may hold values from -3 to 3
- weight: bfloat16 [512, 27, 256], P(('dp', 'tm', 'space')), may hold values from -0.0546875 to 0.0546875
- upstream: bfloat16 [2, 8, 4, 512, 256], P('dp', 'tm', 'space'), may hold values from -20 to 20
Outputs:
- dlatents: bfloat16 [2, 8, 8, 128, 512], P('dp', 'tm', 'space')
- dweight: float32 [512, 27, 256], P(('dp', 'tm', 'space'))
- dgamma: float32 [512], replicated
- dbeta: float32 [512], replicated
The draws below stay inside these ranges and needn't reach their ends.
Inputs may be any that keep to these rules, and one draw needn't show every extreme that they name: `owner`: in every clip each of the 4 owners is named by at most 2 of the 4 tiles, and by exactly 2 in some clips.
All inputs are finite; a program needn't handle non-finite values.
Results may differ from the reference program's by a relative error of at most 0.002.
The reference program's roundings to bfloat16 on the way count: a program that leaves them out, or rounds other values in their place, can miss the bound.
Values may be sent and summed in bfloat16 or wider, within the bound.
No kernel may reach another device: no remote copies, remote signals or barrier semaphores. Data moves between devices by JAX's collectives and lax.ppermute only.
A program may use at most 128 MiB of HBM per device.

```python
import math
import jax
import jax.numpy as jnp
import numpy as np
from jax import lax

C = 512
COUT = 256
GROUPS = 32
TH = 8
TW = 16
GSIZE = 16
CAP = 2
CLIPS = 2
FR = 8
TILES = 4
SLOTS = 8
N_SPACE = 4


def draw_latents(key, part):
    keys = jax.random.split(key, 4)
    shape = (CLIPS, FR, SLOTS, TH * TW, C)
    base = jax.random.normal(keys[0], shape, jnp.float32)
    offset = 0.5 * jax.random.normal(keys[1], (CLIPS, 1, 1, 1, C), jnp.float32)
    frame_scale = 1.0 + 2.0 * jnp.arange(FR, dtype=jnp.float32) / (FR - 1)
    chan_scale = jnp.exp(jax.random.uniform(keys[2], (C,), jnp.float32, -1.2, 1.2))
    slot_scale = jnp.exp(jax.random.uniform(keys[3], (CLIPS, FR, SLOTS, 1, 1), jnp.float32, 0.0, 1.1))
    values = base * frame_scale[None, :, None, None, None] * chan_scale * slot_scale + offset
    return values.astype(jnp.bfloat16)


def draw_upstream(key, part):
    keys = jax.random.split(jax.random.fold_in(key, 77), 2)
    shape = (CLIPS, FR, TILES, 4 * TH * TW, COUT)
    ramp = jnp.arange(FR, dtype=jnp.float32) / (FR - 1)
    base = jnp.clip(jax.random.normal(keys[0], shape, jnp.float32), -4.0, 4.0)
    offset = jnp.clip(0.6 * jax.random.normal(keys[1], (CLIPS, 1, 1, 1, COUT), jnp.float32), -2.0, 2.0)
    frame_scale = 0.4 + 2.0 * ramp
    values = (base + offset) * frame_scale[None, :, None, None, None]
    return values.astype(jnp.bfloat16)


def level_of(stream_key, extent, cuts, smallest, largest):
    def one(dim, parts):
        heights = jax.random.uniform(jax.random.fold_in(jax.random.fold_in(stream_key, 6), dim), (parts,), jnp.float32, smallest / len(cuts), largest / len(cuts))
        return jnp.repeat(jnp.exp(heights), extent[dim] // parts).reshape((-1,) + (1,) * (len(extent) - dim - 1))

    gain = one(*cuts[0])
    for cut in cuts[1:]:
        gain = gain * one(*cut)
    return gain


def shared_out(own_key, own, number, rows, count, top, reach, lean):
    sequence = jax.random.permutation(own_key, count)
    heavy_load, ordinary = load_shares(count, rows * top, reach, lean, True), load_shares(count, rows * top, reach, lean, False)
    places = jnp.arange(count)

    def named(tallies, turn):
        used = int((tallies > 0).sum())
        fixed = max(1, used // 4)
        moved = fixed + (places - fixed + turn * (used - fixed)) % max(1, count - fixed)
        return jnp.zeros((count,), jnp.int32).at[sequence[jnp.where(places < fixed, places, moved)]].set(jnp.asarray(tallies, jnp.int32))

    tallies = jnp.where(number % 4 == 0, named(heavy_load, number // 4), named(ordinary, number - number // 4 - 1))
    mixed = jax.random.permutation(jax.random.fold_in(own, 3), count)
    donor, taker = mixed[0:count // 2 * 2:2], mixed[1:count // 2 * 2:2]
    slack = jnp.minimum(tallies[donor] - 1, reach - tallies[taker]) // 2
    slack = jnp.where((donor == sequence[0]) | (taker == sequence[0]) | (tallies[taker] == 0), 0, jnp.maximum(slack, 0))
    moved = jax.random.randint(jax.random.fold_in(own, 4), (count // 2,), 0, 1 << 20) % (slack + 1)
    tallies = tallies.at[donor].add(-moved).at[taker].add(moved)
    items = jnp.searchsorted(jnp.cumsum(tallies), jnp.arange(rows * top), side="right").astype(jnp.int32)
    grid = items.reshape(top, rows).T
    grid = grid[jax.random.permutation(jax.random.fold_in(own, 1), rows)]
    turn = jax.random.randint(jax.random.fold_in(own, 2), (rows, 1), 0, top)
    return jnp.take_along_axis(grid, (jnp.arange(top)[None, :] + turn) % top, axis=1)


def load_shares(number_of, total, most, skew, full):
    loads = [(1 << 20) // math.isqrt(grade ** skew) + 1 for grade in range(1, number_of + 1)]
    largest = most if full else min(most, max(-(-total // number_of), total * loads[0] // sum(loads)))
    least = 1 if total - largest >= number_of - 1 else 0
    given, spare = [largest] + [least] * (number_of - 1), total - largest - least * (number_of - 1)
    while spare > 0:
        free = [i for i in range(1, number_of) if given[i] < largest] or [i for i in range(1, number_of) if given[i] < most]
        pool, budget = sum([loads[i] for i in free]), spare
        for i in free:
            more = min(most - given[i], max(1, budget * loads[i] // pool), spare)
            given[i] = given[i] + more
            spare = spare - more
    return np.array(given)


def normal_values(rng, dims, deviation, most, shards=(), kind=jnp.bfloat16):
    array = deviation * jax.random.normal(rng, dims, jnp.float32)
    if shards:
        array = array * level_of(rng, dims, shards, -0.22, 0.18)
    return jnp.clip(array, -most, most).astype(kind)


def setup_inputs(seed: int = 0) -> dict:
    seeds = jax.random.split(jax.random.key(seed), 7)
    latents = draw_latents(jax.random.fold_in(seeds[6], 71), 0)
    owner_keys = jax.random.split(jax.random.fold_in(seeds[1], 1), CLIPS * TILES // TILES)
    owner_turns = jax.random.permutation(jax.random.fold_in(seeds[1], 3), CLIPS * TILES // TILES)
    owner = jax.vmap(lambda own, number: shared_out(jax.random.fold_in(seeds[1], 2), own, number, TILES, N_SPACE, 1, CAP, 2))(owner_keys, owner_turns).reshape((CLIPS, TILES, 1))
    gamma = jnp.clip(1.0 + 0.15 * jax.random.normal(seeds[2], (C,), jnp.float32), 0.25, 1.75)
    beta = normal_values(seeds[3], (C,), 0.5, 3.0, (), jnp.float32)
    weight = normal_values(seeds[4], (C, 27, COUT), (27 * C) ** -0.5, 0.0546875, ((0, 32),))
    upstream = draw_upstream(jax.random.fold_in(seeds[6], 71), 0)
    return {"latents": latents, "owner": owner, "gamma": gamma, "beta": beta, "weight": weight, "upstream": upstream}


EPS = 1e-06

def tap_list():
    return [(kt, ky, kx) for kt in range(3) for ky in range(3) for kx in range(3)]

def clip_grads(latent, upper, owned, gamma, beta, weight):
    hot = (owned[:, None] == jnp.arange(N_SPACE, dtype=jnp.int32)[None, :]).astype(jnp.int32)
    rank = lax.optimization_barrier(jnp.sum((jnp.cumsum(hot, axis=0).astype(jnp.int32) - hot) * hot, axis=1)).astype(jnp.int32)
    slot = (owned * CAP + rank).astype(jnp.int32)
    cells = TH * TW
    values = latent[:, slot].astype(jnp.float32)
    grouped = values.reshape(FR, TILES, cells, GROUPS, GSIZE)
    mean = lax.optimization_barrier(jnp.mean(grouped, axis=(0, 1, 2, 4)))
    centred = grouped - mean[:, None]
    var = lax.optimization_barrier(jnp.mean(centred * centred, axis=(0, 1, 2, 4)))
    inverse = lax.rsqrt(var + EPS)
    normed = (centred * inverse[:, None]).reshape(FR, TILES, cells, C)
    act = normed * gamma + beta
    sig = jax.nn.sigmoid(act)
    hidden = (act * sig).astype(jnp.bfloat16)
    pooled = upper.astype(jnp.float32).reshape(FR, TILES, TH, 2, TW, 2, COUT)
    grads = lax.optimization_barrier(jnp.sum(pooled, axis=(3, 5))).reshape(FR, TILES, cells, COUT).astype(jnp.bfloat16)
    extended = jnp.concatenate([hidden[:1], hidden[:1], hidden], axis=0).reshape(FR + 2, TILES, TH, TW, C)
    padded = jnp.pad(extended, ((0, 0), (0, 0), (1, 1), (1, 1), (0, 0)))
    rows = grads.reshape(FR * TILES * cells, COUT)
    terms = []
    dext = jnp.zeros((FR + 2, TILES, TH + 2, TW + 2, C), jnp.float32)
    for index, (kt, ky, kx) in enumerate(tap_list()):
        tap = padded[kt:kt + FR, :, ky:ky + TH, kx:kx + TW].reshape(FR * TILES * cells, C)
        terms.append(lax.dot_general(tap, rows, (((0,), (0,)), ((), ())), preferred_element_type=jnp.float32))
        back = lax.dot_general(rows, weight[:, index, :], (((1,), (1,)), ((), ())), preferred_element_type=jnp.float32)
        dext = dext.at[kt:kt + FR, :, ky:ky + TH, kx:kx + TW].add(back.reshape(FR, TILES, TH, TW, C))
    dweight = jnp.stack(terms, axis=1)
    dinner = dext[:, :, 1:TH + 1, 1:TW + 1].reshape(FR + 2, TILES, cells, C)
    dhidden = dinner[2:]
    dhidden = dhidden.at[0].add(dinner[0] + dinner[1])
    dact = dhidden * (sig * (1.0 + act * (1.0 - sig)))
    dgain = lax.optimization_barrier(jnp.sum(dact * normed, axis=(0, 1, 2)))
    dshift = lax.optimization_barrier(jnp.sum(dact, axis=(0, 1, 2)))
    dnorm = (dact * gamma).reshape(FR, TILES, cells, GROUPS, GSIZE)
    ngroup = normed.reshape(FR, TILES, cells, GROUPS, GSIZE)
    first_m = lax.optimization_barrier(jnp.mean(dnorm, axis=(0, 1, 2, 4)))
    second_m = lax.optimization_barrier(jnp.mean(dnorm * ngroup, axis=(0, 1, 2, 4)))
    dvalues = inverse[:, None] * (dnorm - first_m[:, None] - ngroup * second_m[:, None])
    dfull = dvalues.reshape(FR, TILES, cells, C)
    dfull = dfull.at[..., :COUT].add(grads.astype(jnp.float32))
    dslots = jnp.zeros((FR, SLOTS, cells, C), jnp.bfloat16).at[:, slot].set(dfull.astype(jnp.bfloat16))
    return (dslots, dweight, dgain, dshift)

def reference(latents, owner, gamma, beta, weight, upstream):

    def step(carry, item):
        latent, upper, owned = item
        dslots, dweight, dgain, dshift = clip_grads(latent, upper, owned, gamma, beta, weight)
        return ((carry[0] + dweight, carry[1] + dgain, carry[2] + dshift), dslots)
    start = (jnp.zeros((C, 27, COUT), jnp.float32), jnp.zeros((C,), jnp.float32), jnp.zeros((C,), jnp.float32))
    sums, dlatents = lax.scan(step, start, (latents, upstream, owner[:, :, 0]))
    rscale = 1.0 / math.sqrt(CLIPS * FR * TILES * TH * TW)
    return (dlatents, sums[0] * rscale, sums[1] * rscale, sums[2] * rscale)
```

```python
import math

import jax
import jax.numpy as jnp
from jax import lax
from jax.experimental import pallas as pl
from jax.experimental.pallas import tpu as pltpu
from jax.sharding import PartitionSpec as P

GROUPS = 32
TH = 8
TW = 16


EPS = 1e-06


def shifted(value, axis, steps):
    count = lax.axis_size(axis)
    initial, last = (max(0, -steps), min(count, count - steps))
    return lax.ppermute(value, axis, [(source, source + steps) for source in range(initial, last)])


def tap_list():
    return [(kt, ky, kx) for kt in range(3) for ky in range(3) for kx in range(3)]


def conv_grads(hidden, grads, weight, rscale):
    frames, count, cells, chans = hidden.shape
    outs_ch = grads.shape[3]
    first_dev = lax.axis_index("tm") == 0
    cache = shifted(hidden, "tm", 1)
    repeat = jnp.concatenate([hidden[:1], hidden[:1]], axis=0)
    cache = jnp.where(first_dev, repeat, cache)
    extended = jnp.concatenate([cache, hidden], axis=0).reshape(frames + 2, count, TH, TW, chans)
    padded = jnp.pad(extended, ((0, 0), (0, 0), (1, 1), (1, 1), (0, 0)))
    rows = grads.reshape(frames * count * cells, outs_ch)
    span = lax.axis_size(("dp", "tm", "space")) * weight.shape[0]
    terms = []
    for kt, ky, kx in tap_list():
        tap = padded[kt : kt + frames, :, ky : ky + TH, kx : kx + TW].reshape(
            frames * count * cells, span
        )
        terms.append(
            lax.dot_general(tap, rows, (((0,), (0,)), ((), ())), preferred_element_type=jnp.float32)
        )
    dweight = lax.psum_scatter(
        jnp.stack(terms, axis=1) * rscale, ("dp", "tm", "space"), scatter_dimension=0, tiled=True
    )
    piece = lax.all_gather(weight, ("dp", "tm", "space"), axis=0, tiled=True)
    span = piece.shape[0]
    total = jnp.zeros((frames + 2, count, TH + 2, TW + 2, span), jnp.float32)
    for index, (kt, ky, kx) in enumerate(tap_list()):
        back = lax.dot_general(
            rows, piece[:, index, :], (((1,), (1,)), ((), ())), preferred_element_type=jnp.float32
        )
        total = total.at[kt : kt + frames, :, ky : ky + TH, kx : kx + TW].add(
            back.reshape(frames, count, TH, TW, span)
        )
    dextended = total[:, :, 1 : TH + 1, 1 : TW + 1].reshape(frames + 2, count, cells, span)
    carried = shifted(dextended[:2].astype(jnp.bfloat16), "tm", -1).astype(jnp.float32)
    own_part = dextended[2:]
    own_part = own_part.at[frames - 2 :].add(carried)
    own_part = own_part.at[0].add(jnp.where(first_dev, dextended[0] + dextended[1], 0.0))
    return (own_part, dweight)


def shards(latents, owner, gamma, beta, weight, upstream):
    blocks = latents[0]
    frames, cap, cells, chans = blocks.shape
    spaces = lax.axis_size("space")
    here = lax.axis_index("space")
    per_dev = upstream.shape[2]
    outs_ch = upstream.shape[4]
    tile_ids = owner[0, :, 0]
    tiles = tile_ids.shape[0]
    width = chans // GROUPS
    hot = (tile_ids[:, None] == jnp.arange(spaces, dtype=jnp.int32)[None, :]).astype(jnp.int32)
    rank = jnp.sum((jnp.cumsum(hot, axis=0) - hot) * hot, axis=1)
    slot = tile_ids * cap + rank
    holds = slot[None, :] == (here * cap + jnp.arange(cap, dtype=jnp.int32))[:, None]
    live = jnp.any(holds, axis=1).astype(jnp.float32)
    tile_of = jnp.sum(holds.astype(jnp.int32) * jnp.arange(tiles, dtype=jnp.int32)[None, :], axis=1)
    frames_all = frames * lax.axis_size("tm")
    count = float(frames_all * tiles * cells * width)
    rscale = 1.0 / math.sqrt(lax.axis_size("dp") * frames_all * tiles * cells)
    values = blocks.astype(jnp.float32).reshape(frames, cap, cells, GROUPS, width)
    live_mask = live[None, :, None, None, None]
    total = lax.psum(jnp.sum(values * live_mask, axis=(0, 1, 2, 4)), ("tm", "space"))
    mean = total / count
    centred = values - mean[:, None]
    spread = lax.psum(jnp.sum(centred * centred * live_mask, axis=(0, 1, 2, 4)), ("tm", "space"))
    var = spread / count
    inverse = lax.rsqrt(var + EPS)
    normed = (centred * inverse[:, None]).reshape(frames, cap, cells, chans)
    act = normed * gamma + beta
    sig = jax.nn.sigmoid(act)
    hidden = (act * sig).astype(jnp.bfloat16)
    ups = upstream[0].astype(jnp.float32).reshape(frames, per_dev, TH, 2, TW, 2, outs_ch)
    pooled = jnp.sum(ups, axis=(3, 5)).reshape(frames, per_dev, cells, outs_ch).astype(jnp.bfloat16)
    all_pooled = lax.all_gather(pooled, "space", axis=1, tiled=True)
    live_slot = live[None, :, None, None] > 0.5
    grads = jnp.where(live_slot, all_pooled[:, tile_of], jnp.zeros((), jnp.bfloat16))
    dhidden, dweight = conv_grads(hidden, grads, weight, rscale)
    dact = dhidden * (sig * (1.0 + act * (1.0 - sig))) * live[None, :, None, None]
    dgamma, dbeta = lax.psum(
        (jnp.sum(dact * normed, axis=(0, 1, 2)) * rscale, jnp.sum(dact, axis=(0, 1, 2)) * rscale),
        ("dp", "tm", "space"),
    )
    dnorm = (dact * gamma).reshape(frames, cap, cells, GROUPS, width)
    ngroup = normed.reshape(frames, cap, cells, GROUPS, width)
    first_m, second_m = lax.psum(
        (jnp.sum(dnorm, axis=(0, 1, 2, 4)), jnp.sum(dnorm * ngroup, axis=(0, 1, 2, 4))),
        ("tm", "space"),
    )
    dvalues = inverse[:, None] * (
        dnorm - (first_m / count)[:, None] - ngroup * (second_m / count)[:, None]
    )
    dfull = dvalues.reshape(frames, cap, cells, chans)
    resid = jnp.pad(grads.astype(jnp.float32), ((0, 0), (0, 0), (0, 0), (0, chans - outs_ch)))
    dlatent = ((dfull + resid) * live[None, :, None, None]).astype(jnp.bfloat16)
    return (dlatent[None], dweight, dgamma, dbeta)


LANES = 128
HALF = 2
NZ = 4
NS = 4
CAP = 2

F32 = jnp.float32
BF16 = jnp.bfloat16


def swap(value, axis, mask):
    count = lax.axis_size(axis)
    return lax.ppermute(value, axis, [(i, i ^ mask) for i in range(count)])


def sds(shape, dtype):
    return jax.ShapeDtypeStruct(shape, dtype)


def call(body, outs, ins, scratch=(), name=None):
    return pl.pallas_call(
        body,
        out_shape=outs,
        in_specs=[pl.BlockSpec(memory_space=space) for _, space in ins],
        out_specs=jax.tree.map(lambda _: pl.BlockSpec(memory_space=pltpu.VMEM), outs),
        scratch_shapes=list(scratch),
        compiler_params=pltpu.CompilerParams(vmem_limit_bytes=56 * 1024 * 1024),
        name=name,
    )(*[array for array, _ in ins])


def vm(*arrays):
    return [(a, pltpu.VMEM) for a in arrays]


def pool_body(up_ref, out_ref):
    cells, fine = out_ref.shape[1], up_ref.shape[1]
    q = lax.broadcasted_iota(jnp.int32, (cells, fine), 0)
    p = lax.broadcasted_iota(jnp.int32, (cells, fine), 1)
    coarse = (p >> 6) * TW + ((p & (2 * TW - 1)) >> 1)
    mix = jnp.where(coarse == q, 1.0, 0.0).astype(BF16)
    for f in range(up_ref.shape[0]):
        out_ref[f] = jnp.dot(mix, up_ref[f], preferred_element_type=F32).astype(BF16)


def spread_body(lat_ref, o0, o1, o2, o3, buf):
    here = lax.axis_index("space")
    frames, cap = lat_ref.shape[:2]
    for f in range(frames):
        for c in range(cap):
            buf[...] = lat_ref[f, c].T.reshape(buf.shape)
            for d, out in enumerate((o0, o1, o2, o3)):
                for z in range(NZ):
                    for h in range(HALF):
                        out[z, f, c, h] = buf[h * NZ * NS + z * NS + (here ^ d)]


def ranks(own_ref):
    out = []
    for t in range(own_ref.shape[0]):
        rank = jnp.int32(0)
        for before in range(t):
            rank = rank + jnp.where(own_ref[before] == own_ref[t], 1, 0)
        out.append((own_ref[t], rank))
    return out


def pick_body(own_ref, s0, s1, s2, s3, o0, o1, o2, o3):
    here, zed = lax.axis_index("space"), lax.axis_index("tm")
    frames = s0.shape[1]
    for t, (who, rank) in enumerate(ranks(own_ref)):
        for d, src in enumerate((s0, s1, s2, s3)):

            @pl.when(who == (here ^ d))
            def _(src=src, t=t, rank=rank):
                for e, out in enumerate((o0, o1, o2, o3)):
                    for f in range(frames):
                        out[f, t] = src[zed ^ e, f, rank]


def group_full(rows, top, low):
    return jnp.where(rows < GSZ, top, low)


GSZ = 16


def act_body(q0, q1, q2, q3, ga_ref, be_ref, xh_ref, ds_ref, sh_ref, inv_ref):
    zed = lax.axis_index("tm")
    local, tiles = q0.shape[:2]
    frames = xh_ref.shape[0]
    shape = (HALF * GSZ, LANES)
    rows = lax.broadcasted_iota(jnp.int32, shape, 0)
    lane = lax.broadcasted_iota(jnp.int32, shape, 1)
    count = float(frames * tiles * LANES * GSZ)
    acc = jnp.zeros(shape, F32)
    for e, q in enumerate((q0, q1, q2, q3)):
        for f in range(local):
            for t in range(tiles):
                x = q[f, t].astype(F32).reshape(shape)
                xh_ref[(zed ^ e) * local + f, t] = x
                acc = acc + x
    mean = group_full(rows, jnp.sum(acc[:GSZ]), jnp.sum(acc[GSZ:])) / count

    def spread_of(f, acc):
        for t in range(tiles):
            c = xh_ref[f, t] - mean
            acc = acc + c * c
        return acc

    acc = lax.fori_loop(0, frames, spread_of, jnp.zeros(shape, F32))
    var = group_full(rows, jnp.sum(acc[:GSZ]), jnp.sum(acc[GSZ:])) / count
    inv = lax.rsqrt(var + EPS)
    inv_ref[...] = inv
    gain = ga_ref[...].reshape(shape)
    shift = be_ref[...].reshape(shape)
    col, row = lane & (TW - 1), lane >> 4

    def emit(f, carry):
        for t in range(tiles):
            normed = (xh_ref[f, t] - mean) * inv
            act = normed * gain + shift
            sig = jax.nn.sigmoid(act)
            hid = (act * sig).astype(BF16).astype(F32)
            xh_ref[f, t] = normed
            ds_ref[f, t] = sig * (1.0 + act * (1.0 - sig))
            left = jnp.where(col >= 1, pltpu.roll(hid, 1, 1), 0.0)
            right = jnp.where(col <= TW - 2, pltpu.roll(hid, LANES - 1, 1), 0.0)
            for kx, part in enumerate((left, hid, right)):
                up = jnp.where(row >= 1, pltpu.roll(part, TW, 1), 0.0)
                down = jnp.where(row <= TH - 2, pltpu.roll(part, LANES - TW, 1), 0.0)
                for ky, tap in enumerate((up, part, down)):
                    base = (ky * 3 + kx) * HALF * GSZ
                    sh_ref[f + 2, base : base + HALF * GSZ, t * LANES : (t + 1) * LANES] = tap.astype(BF16)
        return carry

    lax.fori_loop(0, frames, emit, 0)
    sh_ref[0] = sh_ref[2]
    sh_ref[1] = sh_ref[2]


def fetch_grads(pieces, gv, sem):
    here, zed = lax.axis_index("space"), lax.axis_index("tm")
    local = pieces[0].shape[0]
    copies = []
    for flip, group in zip((0, 2, 1, 3), (pieces[0:4], pieces[4:8], pieces[8:12], pieces[12:16])):
        for e, ref in enumerate(group):
            cells = ref.shape[1]
            start = pl.multiple_of((here ^ flip) * cells, cells)
            dst = gv.at[pl.ds((zed ^ e) * local, local), pl.ds(start, cells)]
            copies.append(pltpu.make_async_copy(ref, dst, sem.at[len(copies)]))
    for copy in copies:
        copy.start()
    return copies


def dot_nt(a, b):
    return lax.dot_general(a, b, (((1,), (1,)), ((), ())), preferred_element_type=F32)


def grad_body(wo, wp, xh, ds, ga_ref, inv_ref, *rest):
    pieces, (o0, o1, o2, o3), (gv, wv, dact, res, sem) = rest[:16], rest[16:20], rest[20:]
    zed, clip, here = lax.axis_index("tm"), lax.axis_index("dp"), lax.axis_index("space")
    frames, tiles = xh.shape[:2]
    local = frames // NZ
    taps = wo.shape[0]
    outs_ch = wo.shape[2]
    copies = fetch_grads(pieces, gv, sem)
    for k in range(taps):
        wv[k, clip] = wo[k]
        wv[k, 1 - clip] = wp[k]
    first = (zed * NS + here) * GSZ
    kk = lax.broadcasted_iota(jnp.int32, (GSZ, outs_ch), 0)
    oo = lax.broadcasted_iota(jnp.int32, (GSZ, outs_ch), 1)
    wv[taps, 0] = jnp.where(oo == kk + first, 1.0, 0.0).astype(BF16)
    wv[taps, 1] = jnp.zeros((GSZ, outs_ch), BF16)
    for f in range(frames, frames + 2):
        gv[f] = jnp.zeros(gv.shape[1:], BF16)
    for copy in copies:
        copy.wait()
    shape = (HALF * GSZ, LANES)
    rows = lax.broadcasted_iota(jnp.int32, shape, 0)
    lane = lax.broadcasted_iota(jnp.int32, shape, 1)
    col, row = lane & (TW - 1), lane >> 4
    wide = 9 * HALF * GSZ

    def kernel_of(kt, more=0):
        part = wv[9 * kt : 9 * kt + 9 + more]
        return part.reshape(part.shape[0] * HALF * GSZ, outs_ch)

    def frame(f, sums, extra):
        last = dot_nt(kernel_of(2, 1), gv[f])
        total = last[:wide] + dot_nt(kernel_of(1), gv[f + 1]) + dot_nt(kernel_of(0), gv[f + 2])
        if extra:
            total = total + dot_nt(kernel_of(1), gv[0])
            total = total + dot_nt(kernel_of(0), gv[0])
            total = total + dot_nt(kernel_of(0), gv[1])
        dg, db = sums
        for t in range(tiles):
            tile = total[:, t * LANES : (t + 1) * LANES]
            dh = jnp.zeros(shape, F32)
            for ky in range(3):
                p = [tile[(ky * 3 + kx) * 32 : (ky * 3 + kx + 1) * 32] for kx in range(3)]
                r = p[1]
                r = r + jnp.where(col <= TW - 2, pltpu.roll(p[0], LANES - 1, 1), 0.0)
                r = r + jnp.where(col >= 1, pltpu.roll(p[2], 1, 1), 0.0)
                if ky == 0:
                    r = jnp.where(row <= TH - 2, pltpu.roll(r, LANES - TW, 1), 0.0)
                if ky == 2:
                    r = jnp.where(row >= 1, pltpu.roll(r, TW, 1), 0.0)
                dh = dh + r
            da = dh * ds[f, t]
            dact[f, t] = da
            res[f, t] = last[wide : wide + GSZ, t * LANES : (t + 1) * LANES]
            dg = dg + da * xh[f, t]
            db = db + da
        return dg, db

    sums = frame(0, (jnp.zeros(shape, F32), jnp.zeros(shape, F32)), True)
    dg, db = lax.fori_loop(1, frames, lambda f, s: frame(f, s, False), sums)
    dg = jnp.sum(dg, axis=1, keepdims=True)
    db = jnp.sum(db, axis=1, keepdims=True)
    gain = ga_ref[...].reshape(shape)
    inv = inv_ref[...]
    count = float(frames * tiles * LANES * GSZ)
    gb, gg = gain[:, :1] * db, gain[:, :1] * dg
    m1 = group_full(rows, jnp.sum(gb[:GSZ]), jnp.sum(gb[GSZ:])) / count
    m2 = group_full(rows, jnp.sum(gg[:GSZ]), jnp.sum(gg[GSZ:])) / count
    outs = (o0, o1, o2, o3)
    for e, out in enumerate(outs):
        for f in range(local):
            at = (zed ^ e) * local + f
            for t in range(tiles):
                y = inv * (dact[at, t] * gain - m1 - xh[at, t] * m2)
                y = jnp.concatenate([y[:GSZ] + res[at, t], y[GSZ:]], axis=0)
                out[f * tiles + t] = y.astype(BF16).reshape(HALF, GSZ, LANES)
    rscale = 1.0 / math.sqrt(lax.axis_size("dp") * frames * tiles * LANES)
    block = jnp.zeros(shape, F32)
    at = 0
    for value in (dg * rscale, db * rscale):
        for _ in range(3):
            part = value.astype(BF16).astype(F32)
            block = jnp.where(lane == at, part, block)
            value = value - part
            at += 1
    for out in outs:
        out[local * tiles] = block.astype(BF16).reshape(HALF, GSZ, LANES)


def expand_body(own_ref, p0, p1, p2, p3, o0, o1, o2, o3):
    here, zed = lax.axis_index("space"), lax.axis_index("tm")
    tiles = own_ref.shape[0]
    local = (p0.shape[0] - 1) // tiles
    parts, outs = (p0, p1, p2, p3), (o0, o1, o2, o3)
    for out in outs:
        out[...] = jnp.zeros_like(out)
        for e, part in enumerate(parts):
            out[zed ^ e, local * CAP] = part[local * tiles]
    for t, (who, rank) in enumerate(ranks(own_ref)):
        for d, out in enumerate(outs):

            @pl.when(who == (here ^ d))
            def _(out=out, t=t, rank=rank):
                for e, part in enumerate(parts):
                    for f in range(local):
                        out[zed ^ e, f * CAP + rank] = part[f * tiles + t]


def gather_sums_body(v0, v1, v2, v3, out_ref, buf):
    here = lax.axis_index("space")
    last = v0.shape[1] - 1
    for d, part in enumerate((v0, v1, v2, v3)):
        for z in range(NZ):
            for h in range(HALF):
                buf[h * NZ * NS + z * NS + (here ^ d)] = part[z, last, h].astype(F32)
    wide = buf[...].reshape(-1, LANES).T
    out_ref[...] = jnp.concatenate(
        [
            wide[0:1] + wide[1:2] + wide[2:3],
            wide[3:4] + wide[4:5] + wide[5:6],
            jnp.zeros((6, wide.shape[1]), F32),
        ],
        axis=0,
    )


def collect_body(v0, v1, v2, v3, out_ref, buf):
    here = lax.axis_index("space")
    frames, cap = out_ref.shape[:2]
    for f in range(frames):
        for c in range(cap):
            for d, part in enumerate((v0, v1, v2, v3)):
                for z in range(NZ):
                    for h in range(HALF):
                        buf[h * NZ * NS + z * NS + (here ^ d)] = part[z, f * cap + c, h]
            out_ref[f, c] = buf[...].reshape(-1, LANES).T


def dweight_body(sh_ref, *rest):
    pieces, (keep, send), (gv, acc, sem) = rest[:16], rest[16:18], rest[18:]
    clip = lax.axis_index("dp")
    copies = fetch_grads(pieces, gv, sem)
    frames = gv.shape[0]
    acc[...] = jnp.zeros_like(acc)
    for copy in copies:
        copy.wait()
    rscale = 1.0 / math.sqrt(lax.axis_size("dp") * frames * gv.shape[1])

    def frame(f, carry):
        for kt in range(3):
            part = jnp.dot(sh_ref[f + kt], gv[f], preferred_element_type=F32)
            acc[9 * kt : 9 * kt + 9] += part.reshape(9, HALF, GSZ, part.shape[1])
        return carry

    lax.fori_loop(0, frames, frame, 0)
    for k in range(acc.shape[0]):
        keep[k] = acc[k, clip] * rscale
        send[k] = acc[k, 1 - clip] * rscale


def channel_plan(latents, owner, gamma, beta, weight, upstream):
    lat = latents[0]
    local, cap, cells, chans = lat.shape
    outs_ch = upstream.shape[4]
    tiles = owner.shape[1]
    frames = local * lax.axis_size("tm")
    taps = weight.shape[1]
    slot = lax.axis_index("tm") * NS + lax.axis_index("space")
    own = owner.reshape(tiles)
    anyspace = pl.ANY

    grads = call(
        pool_body,
        sds((local, cells, outs_ch), BF16),
        vm(upstream.reshape(local, 4 * cells, outs_ch)),
        name="pool",
    )
    same = [grads] + [swap(grads, "tm", e) for e in (1, 2, 3)]
    spread = call(
        spread_body,
        [sds((NZ, local, cap, HALF, GSZ, cells), BF16)] * NS,
        vm(lat),
        [pltpu.VMEM((HALF * NZ * NS, GSZ, cells), BF16)],
        name="spread",
    )
    held = [spread[0]] + [swap(spread[d], "space", d) for d in (1, 2, 3)]
    own_w = weight.transpose(1, 0, 2)
    peer_w = swap(own_w, "dp", 1)
    picked = call(
        pick_body,
        [sds((local, tiles, HALF, GSZ, cells), BF16)] * NZ,
        [(own, pltpu.SMEM)] + vm(*held),
        name="pick",
    )
    seen = [picked[0]] + [swap(picked[e], "tm", e) for e in (1, 2, 3)]
    other = [swap(piece, "space", 2) for piece in same]
    pieces = same + other + [swap(piece, "space", 1) for piece in same + other]

    def mine(v):
        rows = lax.dynamic_index_in_dim(v.reshape(HALF, NZ * NS, GSZ), slot, 1, keepdims=False)
        return jnp.broadcast_to(rows[..., None], (HALF, GSZ, LANES))

    gain, shift = mine(gamma), mine(beta)
    wide = HALF * GSZ
    normed, slope, shifts, inv = call(
        act_body,
        [
            sds((frames, tiles, wide, cells), F32),
            sds((frames, tiles, wide, cells), F32),
            sds((frames + 2, 9 * wide, tiles * cells), BF16),
            sds((wide, LANES), F32),
        ],
        vm(*seen, gain, shift),
        name="act",
    )
    shares = call(
        grad_body,
        [sds((local * tiles + 1, HALF, GSZ, cells), BF16)] * NZ,
        vm(own_w, peer_w, normed, slope, gain, inv) + [(p, anyspace) for p in pieces],
        [
            pltpu.VMEM((frames + 2, tiles * cells, outs_ch), BF16),
            pltpu.VMEM((taps + 1, HALF, GSZ, outs_ch), BF16),
            pltpu.VMEM((frames, tiles, wide, cells), F32),
            pltpu.VMEM((frames, tiles, GSZ, cells), F32),
            pltpu.SemaphoreType.DMA((16,)),
        ],
        name="grad",
    )
    back = [shares[0]] + [swap(shares[e], "tm", e) for e in (1, 2, 3)]
    keep, send = call(
        dweight_body,
        [sds((taps, GSZ, outs_ch), F32)] * 2,
        vm(shifts) + [(p, anyspace) for p in pieces],
        [
            pltpu.VMEM((frames, tiles * cells, outs_ch), BF16),
            pltpu.VMEM((taps, HALF, GSZ, outs_ch), F32),
            pltpu.SemaphoreType.DMA((16,)),
        ],
        name="dweight",
    )
    got = swap(send, "dp", 1)
    slots = call(
        expand_body,
        [sds((NZ, local * cap + 1, HALF, GSZ, cells), BF16)] * NS,
        [(own, pltpu.SMEM)] + vm(*back),
        name="expand",
    )
    home = [slots[0]] + [swap(slots[d], "space", d) for d in (1, 2, 3)]
    sums = call(
        gather_sums_body,
        sds((8, chans), F32),
        vm(*home),
        [pltpu.VMEM((HALF * NZ * NS, GSZ, cells), F32)],
        name="sums",
    )
    sums = sums + swap(sums, "dp", 1)
    dlatent = call(
        collect_body,
        sds((local, cap, cells, chans), BF16),
        vm(*home),
        [pltpu.VMEM((HALF * NZ * NS, GSZ, cells), BF16)],
        name="collect",
    )
    dweight = (keep + got).transpose(1, 0, 2)
    return (dlatent[None], dweight, sums[0], sums[1])


def body(latents, owner, gamma, beta, weight, upstream):
    chans = latents.shape[4]
    fits = (
        [lax.axis_size(a) for a in ("dp", "tm", "space")] == [HALF, NZ, NS]
        and weight.shape[0] == GSZ
        and chans == GROUPS * GSZ
        and latents.shape[0] == 1
        and latents.shape[2] == CAP
        and upstream.shape[2] == 1
        and latents.shape[3] == LANES
    )
    plan = channel_plan if fits else shards
    return plan(latents, owner, gamma, beta, weight, upstream)


def solution(mesh):
    return jax.shard_map(
        body,
        mesh=mesh,
        in_specs=(
            P("dp", "tm", "space", None, None),
            P("dp", None, None),
            P(),
            P(),
            P(("dp", "tm", "space"), None, None),
            P("dp", "tm", "space", None, None),
        ),
        out_specs=(
            P("dp", "tm", "space", None, None),
            P(("dp", "tm", "space"), None, None),
            P(),
            P(),
        ),
        check_vma=False,
    )
```

```python
import math

import jax
import jax.numpy as jnp
from jax import lax
from jax.experimental import pallas as pl
from jax.experimental.pallas import tpu as pltpu
from jax.sharding import PartitionSpec as P


GROUPS = 32
TH = 8
TW = 16


EPS = 1e-06


def shifted(value, axis, steps):
    count = lax.axis_size(axis)
    initial, last = (max(0, -steps), min(count, count - steps))
    return lax.ppermute(value, axis, [(source, source + steps) for source in range(initial, last)])


def tap_list():
    return [(kt, ky, kx) for kt in range(3) for ky in range(3) for kx in range(3)]


def conv_grads(hidden, grads, weight, rscale):
    frames, count, cells, chans = hidden.shape
    outs_ch = grads.shape[3]
    first_dev = lax.axis_index("tm") == 0
    cache = shifted(hidden, "tm", 1)
    repeat = jnp.concatenate([hidden[:1], hidden[:1]], axis=0)
    cache = jnp.where(first_dev, repeat, cache)
    extended = jnp.concatenate([cache, hidden], axis=0).reshape(frames + 2, count, TH, TW, chans)
    padded = jnp.pad(extended, ((0, 0), (0, 0), (1, 1), (1, 1), (0, 0)))
    rows = grads.reshape(frames * count * cells, outs_ch)
    span = lax.axis_size(("dp", "tm", "space")) * weight.shape[0]
    terms = []
    for kt, ky, kx in tap_list():
        tap = padded[kt : kt + frames, :, ky : ky + TH, kx : kx + TW].reshape(
            frames * count * cells, span
        )
        terms.append(
            lax.dot_general(tap, rows, (((0,), (0,)), ((), ())), preferred_element_type=jnp.float32)
        )
    dweight = lax.psum_scatter(
        jnp.stack(terms, axis=1) * rscale, ("dp", "tm", "space"), scatter_dimension=0, tiled=True
    )
    piece = lax.all_gather(weight, ("dp", "tm", "space"), axis=0, tiled=True)
    span = piece.shape[0]
    total = jnp.zeros((frames + 2, count, TH + 2, TW + 2, span), jnp.float32)
    for index, (kt, ky, kx) in enumerate(tap_list()):
        back = lax.dot_general(
            rows, piece[:, index, :], (((1,), (1,)), ((), ())), preferred_element_type=jnp.float32
        )
        total = total.at[kt : kt + frames, :, ky : ky + TH, kx : kx + TW].add(
            back.reshape(frames, count, TH, TW, span)
        )
    dextended = total[:, :, 1 : TH + 1, 1 : TW + 1].reshape(frames + 2, count, cells, span)
    carried = shifted(dextended[:2].astype(jnp.bfloat16), "tm", -1).astype(jnp.float32)
    own_part = dextended[2:]
    own_part = own_part.at[frames - 2 :].add(carried)
    own_part = own_part.at[0].add(jnp.where(first_dev, dextended[0] + dextended[1], 0.0))
    return (own_part, dweight)


def shards(latents, owner, gamma, beta, weight, upstream):
    blocks = latents[0]
    frames, cap, cells, chans = blocks.shape
    spaces = lax.axis_size("space")
    here = lax.axis_index("space")
    per_dev = upstream.shape[2]
    outs_ch = upstream.shape[4]
    tile_ids = owner[0, :, 0]
    tiles = tile_ids.shape[0]
    width = chans // GROUPS
    hot = (tile_ids[:, None] == jnp.arange(spaces, dtype=jnp.int32)[None, :]).astype(jnp.int32)
    rank = jnp.sum((jnp.cumsum(hot, axis=0) - hot) * hot, axis=1)
    slot = tile_ids * cap + rank
    holds = slot[None, :] == (here * cap + jnp.arange(cap, dtype=jnp.int32))[:, None]
    live = jnp.any(holds, axis=1).astype(jnp.float32)
    tile_of = jnp.sum(holds.astype(jnp.int32) * jnp.arange(tiles, dtype=jnp.int32)[None, :], axis=1)
    frames_all = frames * lax.axis_size("tm")
    count = float(frames_all * tiles * cells * width)
    rscale = 1.0 / math.sqrt(lax.axis_size("dp") * frames_all * tiles * cells)
    values = blocks.astype(jnp.float32).reshape(frames, cap, cells, GROUPS, width)
    live_mask = live[None, :, None, None, None]
    total = lax.psum(jnp.sum(values * live_mask, axis=(0, 1, 2, 4)), ("tm", "space"))
    mean = total / count
    centred = values - mean[:, None]
    spread = lax.psum(jnp.sum(centred * centred * live_mask, axis=(0, 1, 2, 4)), ("tm", "space"))
    var = spread / count
    inverse = lax.rsqrt(var + EPS)
    normed = (centred * inverse[:, None]).reshape(frames, cap, cells, chans)
    act = normed * gamma + beta
    sig = jax.nn.sigmoid(act)
    hidden = (act * sig).astype(jnp.bfloat16)
    ups = upstream[0].astype(jnp.float32).reshape(frames, per_dev, TH, 2, TW, 2, outs_ch)
    pooled = jnp.sum(ups, axis=(3, 5)).reshape(frames, per_dev, cells, outs_ch).astype(jnp.bfloat16)
    all_pooled = lax.all_gather(pooled, "space", axis=1, tiled=True)
    live_slot = live[None, :, None, None] > 0.5
    grads = jnp.where(live_slot, all_pooled[:, tile_of], jnp.zeros((), jnp.bfloat16))
    dhidden, dweight = conv_grads(hidden, grads, weight, rscale)
    dact = dhidden * (sig * (1.0 + act * (1.0 - sig))) * live[None, :, None, None]
    dgamma, dbeta = lax.psum(
        (jnp.sum(dact * normed, axis=(0, 1, 2)) * rscale, jnp.sum(dact, axis=(0, 1, 2)) * rscale),
        ("dp", "tm", "space"),
    )
    dnorm = (dact * gamma).reshape(frames, cap, cells, GROUPS, width)
    ngroup = normed.reshape(frames, cap, cells, GROUPS, width)
    first_m, second_m = lax.psum(
        (jnp.sum(dnorm, axis=(0, 1, 2, 4)), jnp.sum(dnorm * ngroup, axis=(0, 1, 2, 4))),
        ("tm", "space"),
    )
    dvalues = inverse[:, None] * (
        dnorm - (first_m / count)[:, None] - ngroup * (second_m / count)[:, None]
    )
    dfull = dvalues.reshape(frames, cap, cells, chans)
    resid = jnp.pad(grads.astype(jnp.float32), ((0, 0), (0, 0), (0, 0), (0, chans - outs_ch)))
    dlatent = ((dfull + resid) * live[None, :, None, None]).astype(jnp.bfloat16)
    return (dlatent[None], dweight, dgamma, dbeta)


LANES = 128
HALF = 2
NZ = 4
NS = 4
CAP = 2
GSZ = 16
FIRST_TAPS = 15
WIDE = HALF * GSZ

F32 = jnp.float32
BF16 = jnp.bfloat16
VMEM = pltpu.VMEM


def swap(value, axis, mask):
    count = lax.axis_size(axis)
    return lax.ppermute(value, axis, [(i, i ^ mask) for i in range(count)])


def kernel_step(body, outs, ins, scratch=(), entry=(), limit=24):
    held = [pltpu.with_memory_space_constraint(a, VMEM) for a in ins]
    return pl.pallas_call(
        body,
        out_shape=outs,
        in_specs=[pl.BlockSpec(memory_space=pltpu.HBM)] * len(entry)
        + [pl.BlockSpec(memory_space=VMEM)] * len(held),
        out_specs=jax.tree.map(space_of, outs),
        scratch_shapes=list(scratch),
        compiler_params=pltpu.CompilerParams(vmem_limit_bytes=limit * 1024 * 1024),
    )(*[pltpu.with_memory_space_constraint(a, pltpu.HBM) for a in entry], *held)


def space_of(out):
    return pl.BlockSpec(memory_space=getattr(out, "memory_space", VMEM))


def prep_body(up_hbm, lat_hbm, gamma_hbm, beta_hbm, o0, o1, o2, o3, g_ref, gain, shift, *scratch):
    buf, up_ref, lat_ref, gamma_ref, beta_ref, sem = scratch
    copies = [
        pltpu.make_async_copy(src, dst, sem.at[n])
        for n, (src, dst) in enumerate(
            ((up_hbm, up_ref), (lat_hbm, lat_ref), (gamma_hbm, gamma_ref), (beta_hbm, beta_ref))
        )
    ]
    for copy in copies:
        copy.start()
    here = lax.axis_index("space")
    frames, cap, cells = lat_ref.shape[:3]
    fine = up_ref.shape[1]
    q = lax.broadcasted_iota(jnp.int32, (cells, fine), 0)
    p = lax.broadcasted_iota(jnp.int32, (cells, fine), 1)
    coarse = (p >> 6) * TW + ((p & (2 * TW - 1)) >> 1)
    mix = jnp.where(coarse == q, 1.0, 0.0).astype(BF16)
    slots = NZ * frames * cap * HALF
    copies[0].wait()
    for f in range(frames):
        pooled = jnp.dot(mix, up_ref[f], preferred_element_type=F32).astype(BF16)
        for o in range(pooled.shape[1] // LANES):
            part = pooled[:, o * LANES : (o + 1) * LANES]
            g_ref[f, o] = part
            rows = cells // GSZ
            base = slots + (f * 2 + o) * rows
            o1[base : base + rows] = part.reshape(rows, GSZ, LANES)
            o2[base : base + rows] = part.reshape(rows, GSZ, LANES)
    copies[1].wait()
    for f in range(frames):
        for c in range(cap):
            buf[...] = lat_ref[f, c].T.reshape(buf.shape)
            for d, out in enumerate((o0, o1, o2, o3)):
                for z in range(NZ):
                    for h in range(HALF):
                        at = ((z * frames + f) * cap + c) * HALF + h
                        out[at] = buf[h * NZ * NS + z * NS + (here ^ d)]
    copies[2].wait()
    copies[3].wait()
    slot = lax.axis_index("tm") * NS + here
    gain[...] = jnp.broadcast_to(own_channels(gamma_ref, slot), gain.shape)
    shift[...] = jnp.broadcast_to(own_channels(beta_ref, slot), shift.shape)


def ranks(own_ref):
    out = []
    for t in range(own_ref.shape[0]):
        rank = jnp.int32(0)
        for before in range(t):
            rank = rank + jnp.where(own_ref[before] == own_ref[t], 1, 0)
        out.append((own_ref[t], rank))
    return out


def pick_body(own_hbm, s0, s1, s2, s3, o0, o1, o2, o3, own_ref, sem):
    copy = pltpu.make_async_copy(own_hbm, own_ref, sem)
    copy.start()
    copy.wait()
    here, zed = lax.axis_index("space"), lax.axis_index("tm")
    frames = o0.shape[0]
    for t, (who, rank) in enumerate(ranks(own_ref)):
        for d, src in enumerate((s0, s1, s2, s3)):

            @pl.when(who == (here ^ d))
            def _(src=src, t=t, rank=rank):
                for e, out in enumerate((o0, o1, o2, o3)):
                    for f in range(frames):
                        at = (((zed ^ e) * frames + f) * CAP + rank) * HALF
                        for h in range(HALF):
                            out[f, t, h] = src[at + h]


def join_body(a1, a2, a3, out):
    for e, ref in enumerate((a1, a2, a3)):
        out[e] = ref[...]


def by_group(rows, top, low):
    return jnp.where(rows < GSZ, top, low)


def own_channels(ref, slot):
    count = ref.shape[1]
    k = lax.broadcasted_iota(jnp.int32, (WIDE, count), 0)
    c = lax.broadcasted_iota(jnp.int32, (WIDE, count), 1)
    wanted = (k >> 4) * (count // HALF) + slot * GSZ + (k & (GSZ - 1))
    return jnp.sum(jnp.where(c == wanted, ref[...], 0.0), axis=1, keepdims=True)


def act_body(gain_ref, shift_ref, q0, q1, q2, q3, xh_ref, ds_ref, sh_ref, inv_ref):
    here, zed = lax.axis_index("space"), lax.axis_index("tm")
    local, tiles = q0.shape[:2]
    frames = xh_ref.shape[0]
    shape = (WIDE, LANES)
    rows = lax.broadcasted_iota(jnp.int32, shape, 0)
    lane = lax.broadcasted_iota(jnp.int32, shape, 1)
    count = float(frames * tiles * LANES * GSZ)
    acc = jnp.zeros(shape, F32)
    for e, q in enumerate((q0, q1, q2, q3)):
        for f in range(local):
            for t in range(tiles):
                x = q[f, here ^ t].astype(F32).reshape(shape)
                xh_ref[(zed ^ e) * local + f, t] = x
                acc = acc + x
    mean = by_group(rows, jnp.sum(acc[:GSZ]), jnp.sum(acc[GSZ:])) / count

    def spread_of(f, acc):
        for t in range(tiles):
            c = xh_ref[f, t] - mean
            acc = acc + c * c
        return acc

    acc = lax.fori_loop(0, frames, spread_of, jnp.zeros(shape, F32))
    var = by_group(rows, jnp.sum(acc[:GSZ]), jnp.sum(acc[GSZ:])) / count
    inv = lax.rsqrt(var + EPS)
    gain, shift = gain_ref[...], shift_ref[...]
    inv_ref[...] = inv
    col, row = lane & (TW - 1), lane >> 4

    def emit(f, carry):
        for t in range(tiles):
            normed = (xh_ref[f, t] - mean) * inv
            act = normed * gain + shift
            sig = jax.nn.sigmoid(act)
            hid = (act * sig).astype(BF16).astype(F32)
            xh_ref[f, t] = normed
            ds_ref[f, t] = sig * (1.0 + act * (1.0 - sig))
            left = jnp.where(col >= 1, pltpu.roll(hid, 1, 1), 0.0)
            right = jnp.where(col <= TW - 2, pltpu.roll(hid, LANES - 1, 1), 0.0)
            for kx, part in enumerate((left, hid, right)):
                up = jnp.where(row >= 1, pltpu.roll(part, TW, 1), 0.0)
                down = jnp.where(row <= TH - 2, pltpu.roll(part, LANES - TW, 1), 0.0)
                for ky, tap in enumerate((up, part, down)):
                    tap = tap.astype(BF16)
                    base = (ky * 3 + kx) * GSZ
                    for h in range(HALF):
                        sh_ref[f + 2, h, base : base + GSZ, t * LANES : (t + 1) * LANES] = tap[
                            h * GSZ : (h + 1) * GSZ
                        ]
        return carry

    lax.fori_loop(0, frames, emit, 0)
    sh_ref[0] = sh_ref[2]
    sh_ref[1] = sh_ref[2]


def place(gv, row, own, rest):
    zed = lax.axis_index("tm")
    local, cells = rest.shape[1], rest.shape[3]
    steps = cells // GSZ
    rows = slice(row, row + cells)
    for f in range(local):
        for o in range(2):
            lanes = slice(o * LANES, (o + 1) * LANES)
            if len(own.shape) == 3:
                at = own.shape[0] - (local * 2 - f * 2 - o) * steps
                gv[zed * local + f, rows, lanes] = own[at : at + steps].reshape(cells, LANES)
            else:
                gv[zed * local + f, rows, lanes] = own[f, o]
            for e in (1, 2, 3):
                gv[(zed ^ e) * local + f, rows, lanes] = rest[e - 1, f, o]
    frames = local * NZ
    for f in range(frames, frames + 2):
        gv[f, rows] = jnp.zeros((cells, gv.shape[2]), BF16)


def dot_nt(a, b):
    return lax.dot_general(a, b, (((1,), (1,)), ((), ())), preferred_element_type=F32)


def unshift(p, col, row):
    out = None
    for ky in range(3):
        part = [p[(ky * 3 + kx) * WIDE : (ky * 3 + kx + 1) * WIDE] for kx in range(3)]
        r = part[1]
        r = r + jnp.where(col <= TW - 2, pltpu.roll(part[0], LANES - 1, 1), 0.0)
        r = r + jnp.where(col >= 1, pltpu.roll(part[2], 1, 1), 0.0)
        if ky == 0:
            r = jnp.where(row <= TH - 2, pltpu.roll(r, LANES - TW, 1), 0.0)
        if ky == 2:
            r = jnp.where(row >= 1, pltpu.roll(r, TW, 1), 0.0)
        out = r if out is None else out + r
    return out


def hidden_grads(wv, gv, row, tiles, dh, res):
    shape = (WIDE, LANES)
    lane = lax.broadcasted_iota(jnp.int32, shape, 1)
    col, line = lane & (TW - 1), lane >> 4
    outs_ch = gv.shape[2]
    wide = 9 * WIDE
    frames = gv.shape[0] - 2
    step = 4 // tiles
    rows = slice(row, row + tiles * LANES)

    def kernel_of(kt, more=0):
        part = wv[9 * kt : 9 * kt + 9 + more]
        return part.reshape(part.shape[0] * WIDE, outs_ch)

    def grads_at(f, n=step):
        return gv[pl.ds(f, n), rows].reshape(n * tiles * LANES, outs_ch)

    def group(f, first):
        last = dot_nt(kernel_of(2, 1), grads_at(f))
        total = last[:wide] + dot_nt(kernel_of(1), grads_at(f + 1)) + dot_nt(kernel_of(0), grads_at(f + 2))
        extra = None
        if first:
            extra = dot_nt(kernel_of(1), grads_at(0, 1)) + dot_nt(kernel_of(0), grads_at(0, 1))
            extra = extra + dot_nt(kernel_of(0), grads_at(1, 1))
        for n in range(step):
            for t in range(tiles):
                at = (n * tiles + t) * LANES
                p = total[:, at : at + LANES]
                if first and n == 0:
                    p = p + extra[:, t * LANES : (t + 1) * LANES]
                dh[f + n, t] = unshift(p, col, line)
                res[f + n, t] = last[wide : wide + GSZ, at : at + LANES]

    group(0, True)

    def later(n, carry):
        group(n * step, False)
        return carry

    lax.fori_loop(1, frames // step, later, 0)


def grad_near_body(wo, wp, g, a3, r1, c3, wv, gv, dh, res):
    zed, clip, here = lax.axis_index("tm"), lax.axis_index("dp"), lax.axis_index("space")
    taps, outs_ch = wo.shape[0], wo.shape[2]
    for k in range(taps):
        wv[k, clip] = wo[k]
        wv[k, 1 - clip] = wp[k]
    first = (zed * NS + here) * GSZ
    kk = lax.broadcasted_iota(jnp.int32, (GSZ, outs_ch), 0)
    oo = lax.broadcasted_iota(jnp.int32, (GSZ, outs_ch), 1)
    wv[taps, 0] = jnp.where(oo == kk + first, 1.0, 0.0).astype(BF16)
    wv[taps, 1] = jnp.zeros((GSZ, outs_ch), BF16)
    place(gv, 0, g, a3)
    place(gv, LANES, r1, c3)
    hidden_grads(wv, gv, 0, 2, dh, res)


def grad_far_body(wv, r2, y3, gv, dh, res):
    place(gv, 0, r2, y3)
    hidden_grads(wv, gv, 0, 1, dh, res)


def grad_last_body(wv, gv2, d0, d3, dh01, res01, dh2, res2, xh, ds, gain_ref, inv_ref, *rest):
    (o0, o1, o2, o3, gv), (dh3, res3, dact) = rest[:5], rest[5:]
    here, zed = lax.axis_index("space"), lax.axis_index("tm")
    frames, tiles = xh.shape[:2]
    local = frames // NZ
    gv[:, :LANES] = gv2[...]
    place(gv, LANES, d0, d3)
    hidden_grads(wv, gv, LANES, 1, dh3, res3)
    shape = (WIDE, LANES)
    rows = lax.broadcasted_iota(jnp.int32, shape, 0)
    lane = lax.broadcasted_iota(jnp.int32, shape, 1)
    parts = ((dh01, res01, 0), (dh01, res01, 1), (dh2, res2, 0), (dh3, res3, 0))

    def sums_of(f, sums):
        dg, db = sums
        for t, (dh, _, at) in enumerate(parts):
            da = dh[f, at] * ds[f, t]
            dact[f, t] = da
            dg = dg + da * xh[f, t]
            db = db + da
        return dg, db

    zero = jnp.zeros(shape, F32)
    dg, db = lax.fori_loop(0, frames, sums_of, (zero, zero))
    dg = jnp.sum(dg, axis=1, keepdims=True)
    db = jnp.sum(db, axis=1, keepdims=True)
    gain = gain_ref[...]
    inv = inv_ref[...]
    count = float(frames * tiles * LANES * GSZ)
    gb, gg = gain[:, :1] * db, gain[:, :1] * dg
    m1 = by_group(rows, jnp.sum(gb[:GSZ]), jnp.sum(gb[GSZ:])) / count
    m2 = by_group(rows, jnp.sum(gg[:GSZ]), jnp.sum(gg[GSZ:])) / count
    outs = (o0, o1, o2, o3)
    for e, out in enumerate(outs):
        for f in range(local):
            frame = (zed ^ e) * local + f
            for t, (_, res, at) in enumerate(parts):
                y = inv * (dact[frame, t] * gain - m1 - xh[frame, t] * m2)
                base = (f * tiles + (here ^ t)) * HALF
                out[base] = (y[:GSZ] + res[frame, at]).astype(BF16)
                out[base + 1] = y[GSZ:].astype(BF16)
    rscale = 1.0 / math.sqrt(lax.axis_size("dp") * frames * tiles * LANES)
    spot = lane == zed * WIDE + rows
    line = lax.broadcasted_iota(jnp.int32, (GSZ, LANES), 0)
    block = jnp.zeros((GSZ, LANES), F32)
    at = 0
    for value in (dg, db):
        value = jnp.sum(jnp.where(spot, value * rscale, 0.0), axis=0, keepdims=True)
        for _ in range(3):
            part = value.astype(BF16).astype(F32)
            block = jnp.where(line == at, part, block)
            value = value - part
            at += 1
    for out in outs:
        out[local * tiles * HALF] = block.astype(BF16)


def dweight_body(flip, sh_ref, near, far, *rest):
    outs, acc = rest[:-1], rest[-1]
    half = lax.axis_index("dp") ^ flip
    frames = near.shape[0] - 2
    pair = near.shape[1]
    acc[...] = jnp.zeros_like(acc)

    def frame(f, carry):
        taps = sh_ref[pl.ds(f, 3), half].reshape(acc.shape[0], 2 * pair)
        part = jnp.dot(taps[:, :pair], near[f], preferred_element_type=F32)
        acc[...] += part + jnp.dot(taps[:, pair:], far[f], preferred_element_type=F32)
        return carry

    lax.fori_loop(0, frames, frame, 0)
    rscale = 1.0 / math.sqrt(lax.axis_size("dp") * frames * 2 * pair)
    total = (acc[...] * rscale).reshape(-1, GSZ, acc.shape[1])
    start = 0
    for out in outs:
        out[...] = total[start : start + out.shape[0]]
        start += out.shape[0]


def expand_body(own_hbm, p0, p1, p2, p3, o0, o1, o2, o3, sums, own_ref, sem):
    copy = pltpu.make_async_copy(own_hbm, own_ref, sem)
    copy.start()
    here, zed = lax.axis_index("space"), lax.axis_index("tm")
    tiles = own_hbm.shape[0]
    local = (p0.shape[0] - 1) // tiles // HALF
    parts, outs = (p0, p1, p2, p3), (o0, o1, o2, o3)
    for out in outs:
        out[...] = jnp.zeros_like(out)
    block = jnp.zeros((GSZ, LANES), F32)
    for part in parts:
        block = block + part[local * tiles * HALF].astype(F32)
    sums[0:1] = block[0:1] + block[1:2] + block[2:3]
    sums[1:2] = block[3:4] + block[4:5] + block[5:6]
    sums[2:8] = jnp.zeros((6, LANES), F32)
    copy.wait()
    for t, (who, rank) in enumerate(ranks(own_ref)):
        for d, out in enumerate(outs):

            @pl.when(who == (here ^ d))
            def _(out=out, t=t, rank=rank):
                for e, part in enumerate(parts):
                    for f in range(local):
                        at = (((zed ^ e) * local + f) * CAP + rank) * HALF
                        base = (f * tiles + t) * HALF
                        for h in range(HALF):
                            out[at + h] = part[base + h]


def mix_body(mine, peer, out):
    out[...] = mine[...] + peer[...]


def collect_body(v0, v1, v2, v3, s0, s1, s2, s3, out_ref, dg_ref, db_ref, buf):
    here = lax.axis_index("space")
    frames, cap = out_ref.shape[:2]
    for f in range(frames):
        for c in range(cap):
            for d, part in enumerate((v0, v1, v2, v3)):
                for z in range(NZ):
                    for h in range(HALF):
                        at = ((z * frames + f) * cap + c) * HALF + h
                        buf[h * NZ * NS + z * NS + (here ^ d)] = part[at]
            out_ref[f, c] = buf[...].reshape(-1, LANES).T
    chans = dg_ref.shape[1]
    lane = lax.broadcasted_iota(jnp.int32, (LANES, chans), 0)
    chan = lax.broadcasted_iota(jnp.int32, (LANES, chans), 1)
    z, h, k = lane >> 5, (lane >> 4) & 1, lane & (GSZ - 1)
    total = jnp.zeros((8, chans), F32)
    for d, part in enumerate((s0, s1, s2, s3)):
        goal = h * (chans // HALF) + z * (NS * GSZ) + (here ^ d) * GSZ + k
        sort = jnp.where(chan == goal, 1.0, 0.0)
        total = total + jnp.dot(
            part[...], sort, precision=lax.Precision.HIGHEST, preferred_element_type=F32
        )
    dg_ref[...] = total[0:1]
    db_ref[...] = total[1:2]


def total_body(keep, got1, got2, out):
    first = got1.shape[0]
    out[:first] = keep[:first] + got1[...]
    out[first:] = keep[first:] + got2[...]


def channel_plan(latents, owner, gamma, beta, weight, upstream):
    lat = latents[0]
    local, cap, cells, chans = lat.shape
    outs_ch = upstream.shape[4]
    tiles = owner.shape[1]
    frames = local * lax.axis_size("tm")
    taps = weight.shape[1]
    own = owner.reshape(tiles)
    slots = NZ * local * cap * HALF
    more = local * outs_ch // LANES * cells // GSZ
    own_w = weight.transpose(1, 0, 2)

    spread = [slots, slots + more, slots + more, slots]
    t0, t1, t2, t3, grads, gain, shift = kernel_step(
        prep_body,
        [VMEM((count, GSZ, cells), BF16) for count in spread]
        + [
            VMEM((local, outs_ch // LANES, cells, LANES), BF16),
            VMEM((WIDE, LANES), F32),
            VMEM((WIDE, LANES), F32),
        ],
        [],
        [
            VMEM((HALF * NZ * NS, GSZ, cells), BF16),
            VMEM((local, 4 * cells, outs_ch), BF16),
            VMEM(lat.shape, BF16),
            VMEM((1, chans), F32),
            VMEM((1, chans), F32),
            pltpu.SemaphoreType.DMA((4,)),
        ],
        entry=(
            upstream.reshape(local, 4 * cells, outs_ch),
            lat,
            gamma.reshape(1, chans),
            beta.reshape(1, chans),
        ),
    )
    along = [swap(grads, "tm", e) for e in (1, 2, 3)]
    r2, r3, r1 = (swap(v, "space", d) for v, d in ((t2, 2), (t3, 3), (t1, 1)))
    peer_w = swap(own_w, "dp", 1)
    d0 = swap(r2, "space", 1)
    owner_scratch = [pltpu.SMEM((tiles,), jnp.int32), pltpu.SemaphoreType.DMA]
    picked = kernel_step(
        pick_body,
        [VMEM((local, tiles, HALF, GSZ, cells), BF16)] * NZ,
        [t0, r1, r2, r3],
        owner_scratch,
        entry=(own,),
    )
    seen = [picked[0]] + [swap(picked[e], "tm", e) for e in (1, 2, 3)]
    a3 = kernel_step(join_body, VMEM((3,) + grads.shape, BF16), along)
    y3, c3 = swap(a3, "space", 2), swap(a3, "space", 1)
    d3 = swap(y3, "space", 1)
    normed, slope, shifts, inv = kernel_step(
        act_body,
        [
            VMEM((frames, tiles, WIDE, cells), F32),
            VMEM((frames, tiles, WIDE, cells), F32),
            VMEM((frames + 2, HALF, 9 * GSZ, tiles * cells), BF16),
            VMEM((WIDE, LANES), F32),
        ],
        [gain, shift] + seen,
    )

    def hidden_shapes(count):
        return [VMEM((frames, count, WIDE, cells), F32), VMEM((frames, count, GSZ, cells), F32)]

    taps_all, near, dh01, res01 = kernel_step(
        grad_near_body,
        [
            VMEM((taps + 1, HALF, GSZ, outs_ch), BF16),
            VMEM((frames + 2, 2 * cells, outs_ch), BF16),
        ]
        + hidden_shapes(2),
        [own_w, peer_w, grads, a3, r1, c3],
    )
    far2, dh2, res2 = kernel_step(
        grad_far_body,
        [VMEM((frames + 2, cells, outs_ch), BF16)] + hidden_shapes(1),
        [taps_all, r2, y3],
    )
    shares = kernel_step(
        grad_last_body,
        [VMEM((local * tiles * HALF + 1, GSZ, cells), BF16)] * NZ
        + [VMEM((frames + 2, 2 * cells, outs_ch), BF16)],
        [taps_all, far2, d0, d3, dh01, res01, dh2, res2, normed, slope, gain, inv],
        hidden_shapes(1) + [VMEM((frames, tiles, WIDE, cells), F32)],
    )
    far = shares[4]
    back = [shares[0]] + [swap(shares[e], "tm", e) for e in (1, 2, 3)]

    def dweight_half(flip, *parts):
        return kernel_step(
            lambda *refs: dweight_body(flip, *refs),
            [VMEM((part, GSZ, outs_ch), F32) for part in parts],
            [shifts, near, far],
            [VMEM((taps * GSZ, outs_ch), F32)],
        )

    send1, send2 = dweight_half(1, FIRST_TAPS, taps - FIRST_TAPS)
    got1, got2 = swap(send1, "dp", 1), swap(send2, "dp", 1)
    *spots, sums = kernel_step(
        expand_body,
        [VMEM((slots, GSZ, cells), BF16)] * NS + [VMEM((8, LANES), F32)],
        back,
        owner_scratch,
        entry=(own,),
    )
    home = [spots[0]] + [swap(spots[d], "space", d) for d in (1, 2, 3)]
    (keep,) = dweight_half(0, taps)
    dweight = kernel_step(
        total_body, jax.ShapeDtypeStruct((taps, GSZ, outs_ch), F32), [keep, got1, got2]
    )
    mixed = kernel_step(mix_body, VMEM((8, LANES), F32), [sums, swap(sums, "dp", 1)])
    mixes = [mixed] + [swap(mixed, "space", d) for d in (1, 2, 3)]
    dlatent, dgamma, dbeta = kernel_step(
        collect_body,
        [
            jax.ShapeDtypeStruct((local, cap, cells, chans), BF16),
            jax.ShapeDtypeStruct((1, chans), F32),
            jax.ShapeDtypeStruct((1, chans), F32),
        ],
        home + mixes,
        [VMEM((HALF * NZ * NS, GSZ, cells), BF16)],
    )
    return (dlatent[None], dweight.transpose(1, 0, 2), dgamma.reshape(chans), dbeta.reshape(chans))


def fits_plan(sizes, latents, weight, upstream):
    return (
        sizes == [HALF, NZ, NS]
        and weight.shape[0] == GSZ
        and latents.shape[4] == GROUPS * GSZ
        and latents.shape[0] == 1
        and latents.shape[2] == CAP
        and upstream.shape[2] == 1
        and latents.shape[3] == LANES
    )


def body(latents, owner, gamma, beta, weight, upstream):
    args = (latents, owner, gamma, beta, weight, upstream)
    sizes = [lax.axis_size(a) for a in ("dp", "tm", "space")]
    if not fits_plan(sizes, latents, weight, upstream):
        return shards(*args)
    return channel_plan(*args)


def solution(mesh):
    return jax.shard_map(
        body,
        mesh=mesh,
        in_specs=(
            P("dp", "tm", "space", None, None),
            P("dp", None, None),
            P(),
            P(),
            P(("dp", "tm", "space"), None, None),
            P("dp", "tm", "space", None, None),
        ),
        out_specs=(
            P("dp", "tm", "space", None, None),
            P(("dp", "tm", "space"), None, None),
            P(),
            P(),
        ),
        check_vma=False,
    )
```

```python
import math

import jax
import jax.numpy as jnp
from jax import lax
from jax.experimental import pallas as pl
from jax.experimental.pallas import tpu as pltpu
from jax.sharding import PartitionSpec as P


GROUPS = 32
TH = 8
TW = 16


EPS = 1e-06


def shifted(value, axis, steps):
    count = lax.axis_size(axis)
    initial, last = (max(0, -steps), min(count, count - steps))
    return lax.ppermute(value, axis, [(source, source + steps) for source in range(initial, last)])


def tap_list():
    return [(kt, ky, kx) for kt in range(3) for ky in range(3) for kx in range(3)]


def conv_grads(hidden, grads, weight, rscale):
    frames, count, cells, chans = hidden.shape
    outs_ch = grads.shape[3]
    first_dev = lax.axis_index("tm") == 0
    cache = shifted(hidden, "tm", 1)
    repeat = jnp.concatenate([hidden[:1], hidden[:1]], axis=0)
    cache = jnp.where(first_dev, repeat, cache)
    extended = jnp.concatenate([cache, hidden], axis=0).reshape(frames + 2, count, TH, TW, chans)
    padded = jnp.pad(extended, ((0, 0), (0, 0), (1, 1), (1, 1), (0, 0)))
    rows = grads.reshape(frames * count * cells, outs_ch)
    span = lax.axis_size(("dp", "tm", "space")) * weight.shape[0]
    terms = []
    for kt, ky, kx in tap_list():
        tap = padded[kt : kt + frames, :, ky : ky + TH, kx : kx + TW].reshape(
            frames * count * cells, span
        )
        terms.append(
            lax.dot_general(tap, rows, (((0,), (0,)), ((), ())), preferred_element_type=jnp.float32)
        )
    dweight = lax.psum_scatter(
        jnp.stack(terms, axis=1) * rscale, ("dp", "tm", "space"), scatter_dimension=0, tiled=True
    )
    piece = lax.all_gather(weight, ("dp", "tm", "space"), axis=0, tiled=True)
    span = piece.shape[0]
    total = jnp.zeros((frames + 2, count, TH + 2, TW + 2, span), jnp.float32)
    for index, (kt, ky, kx) in enumerate(tap_list()):
        back = lax.dot_general(
            rows, piece[:, index, :], (((1,), (1,)), ((), ())), preferred_element_type=jnp.float32
        )
        total = total.at[kt : kt + frames, :, ky : ky + TH, kx : kx + TW].add(
            back.reshape(frames, count, TH, TW, span)
        )
    dextended = total[:, :, 1 : TH + 1, 1 : TW + 1].reshape(frames + 2, count, cells, span)
    carried = shifted(dextended[:2].astype(jnp.bfloat16), "tm", -1).astype(jnp.float32)
    own_part = dextended[2:]
    own_part = own_part.at[frames - 2 :].add(carried)
    own_part = own_part.at[0].add(jnp.where(first_dev, dextended[0] + dextended[1], 0.0))
    return (own_part, dweight)


def shards(latents, owner, gamma, beta, weight, upstream):
    blocks = latents[0]
    frames, cap, cells, chans = blocks.shape
    spaces = lax.axis_size("space")
    here = lax.axis_index("space")
    per_dev = upstream.shape[2]
    outs_ch = upstream.shape[4]
    tile_ids = owner[0, :, 0]
    tiles = tile_ids.shape[0]
    width = chans // GROUPS
    hot = (tile_ids[:, None] == jnp.arange(spaces, dtype=jnp.int32)[None, :]).astype(jnp.int32)
    rank = jnp.sum((jnp.cumsum(hot, axis=0) - hot) * hot, axis=1)
    slot = tile_ids * cap + rank
    holds = slot[None, :] == (here * cap + jnp.arange(cap, dtype=jnp.int32))[:, None]
    live = jnp.any(holds, axis=1).astype(jnp.float32)
    tile_of = jnp.sum(holds.astype(jnp.int32) * jnp.arange(tiles, dtype=jnp.int32)[None, :], axis=1)
    frames_all = frames * lax.axis_size("tm")
    count = float(frames_all * tiles * cells * width)
    rscale = 1.0 / math.sqrt(lax.axis_size("dp") * frames_all * tiles * cells)
    values = blocks.astype(jnp.float32).reshape(frames, cap, cells, GROUPS, width)
    live_mask = live[None, :, None, None, None]
    total = lax.psum(jnp.sum(values * live_mask, axis=(0, 1, 2, 4)), ("tm", "space"))
    mean = total / count
    centred = values - mean[:, None]
    spread = lax.psum(jnp.sum(centred * centred * live_mask, axis=(0, 1, 2, 4)), ("tm", "space"))
    var = spread / count
    inverse = lax.rsqrt(var + EPS)
    normed = (centred * inverse[:, None]).reshape(frames, cap, cells, chans)
    act = normed * gamma + beta
    sig = jax.nn.sigmoid(act)
    hidden = (act * sig).astype(jnp.bfloat16)
    ups = upstream[0].astype(jnp.float32).reshape(frames, per_dev, TH, 2, TW, 2, outs_ch)
    pooled = jnp.sum(ups, axis=(3, 5)).reshape(frames, per_dev, cells, outs_ch).astype(jnp.bfloat16)
    all_pooled = lax.all_gather(pooled, "space", axis=1, tiled=True)
    live_slot = live[None, :, None, None] > 0.5
    grads = jnp.where(live_slot, all_pooled[:, tile_of], jnp.zeros((), jnp.bfloat16))
    dhidden, dweight = conv_grads(hidden, grads, weight, rscale)
    dact = dhidden * (sig * (1.0 + act * (1.0 - sig))) * live[None, :, None, None]
    dgamma, dbeta = lax.psum(
        (jnp.sum(dact * normed, axis=(0, 1, 2)) * rscale, jnp.sum(dact, axis=(0, 1, 2)) * rscale),
        ("dp", "tm", "space"),
    )
    dnorm = (dact * gamma).reshape(frames, cap, cells, GROUPS, width)
    ngroup = normed.reshape(frames, cap, cells, GROUPS, width)
    first_m, second_m = lax.psum(
        (jnp.sum(dnorm, axis=(0, 1, 2, 4)), jnp.sum(dnorm * ngroup, axis=(0, 1, 2, 4))),
        ("tm", "space"),
    )
    dvalues = inverse[:, None] * (
        dnorm - (first_m / count)[:, None] - ngroup * (second_m / count)[:, None]
    )
    dfull = dvalues.reshape(frames, cap, cells, chans)
    resid = jnp.pad(grads.astype(jnp.float32), ((0, 0), (0, 0), (0, 0), (0, chans - outs_ch)))
    dlatent = ((dfull + resid) * live[None, :, None, None]).astype(jnp.bfloat16)
    return (dlatent[None], dweight, dgamma, dbeta)


LANES = 128
HALF = 2
NZ = 4
NS = 4
CAP = 2
GSZ = 16
FIRST_TAPS = 18
WIDE = HALF * GSZ

F32 = jnp.float32
BF16 = jnp.bfloat16
VMEM = pltpu.VMEM


def swap(value, axis, mask):
    count = lax.axis_size(axis)
    return lax.ppermute(value, axis, [(i, i ^ mask) for i in range(count)])


def kernel_step(body, outs, ins, scratch=(), entry=(), limit=24):
    held = [pltpu.with_memory_space_constraint(a, VMEM) for a in ins]
    return pl.pallas_call(
        body,
        out_shape=outs,
        in_specs=[pl.BlockSpec(memory_space=pltpu.HBM)] * len(entry)
        + [pl.BlockSpec(memory_space=VMEM)] * len(held),
        out_specs=jax.tree.map(space_of, outs),
        scratch_shapes=list(scratch),
        compiler_params=pltpu.CompilerParams(vmem_limit_bytes=limit * 1024 * 1024),
    )(*[pltpu.with_memory_space_constraint(a, pltpu.HBM) for a in entry], *held)


def space_of(out):
    return pl.BlockSpec(memory_space=getattr(out, "memory_space", VMEM))


def prep_body(up_hbm, lat_hbm, gamma_hbm, beta_hbm, o0, o1, o2, o3, g_ref, gain, shift, *scratch):
    buf, up_ref, lat_ref, gamma_ref, beta_ref, sem = scratch
    copies = [
        pltpu.make_async_copy(src, dst, sem.at[n])
        for n, (src, dst) in enumerate(
            ((up_hbm, up_ref), (lat_hbm, lat_ref), (gamma_hbm, gamma_ref), (beta_hbm, beta_ref))
        )
    ]
    for copy in copies:
        copy.start()
    here = lax.axis_index("space")
    frames, cap, cells = lat_ref.shape[:3]
    fine = up_ref.shape[1]
    q = lax.broadcasted_iota(jnp.int32, (cells, fine), 0)
    p = lax.broadcasted_iota(jnp.int32, (cells, fine), 1)
    coarse = (p >> 6) * TW + ((p & (2 * TW - 1)) >> 1)
    mix = jnp.where(coarse == q, 1.0, 0.0).astype(BF16)
    slots = NZ * frames * cap * HALF
    copies[0].wait()
    for f in range(frames):
        pooled = jnp.dot(mix, up_ref[f], preferred_element_type=F32).astype(BF16)
        for o in range(pooled.shape[1] // LANES):
            part = pooled[:, o * LANES : (o + 1) * LANES]
            g_ref[f, o] = part
            rows = cells // GSZ
            base = slots + (f * 2 + o) * rows
            o1[base : base + rows] = part.reshape(rows, GSZ, LANES)
            o2[base : base + rows] = part.reshape(rows, GSZ, LANES)
    copies[1].wait()
    for f in range(frames):
        for c in range(cap):
            buf[...] = lat_ref[f, c].T.reshape(buf.shape)
            for d, out in enumerate((o0, o1, o2, o3)):
                for z in range(NZ):
                    for h in range(HALF):
                        at = ((z * frames + f) * cap + c) * HALF + h
                        out[at] = buf[h * NZ * NS + z * NS + (here ^ d)]
    copies[2].wait()
    copies[3].wait()
    slot = lax.axis_index("tm") * NS + here
    gain[...] = jnp.broadcast_to(own_channels(gamma_ref, slot), gain.shape)
    shift[...] = jnp.broadcast_to(own_channels(beta_ref, slot), shift.shape)


def ranks(own_ref):
    out = []
    for t in range(own_ref.shape[0]):
        rank = jnp.int32(0)
        for before in range(t):
            rank = rank + jnp.where(own_ref[before] == own_ref[t], 1, 0)
        out.append((own_ref[t], rank))
    return out


def pick_body(own_hbm, s0, s1, s2, s3, o0, o1, o2, o3, own_ref, sem):
    copy = pltpu.make_async_copy(own_hbm, own_ref, sem)
    copy.start()
    copy.wait()
    here, zed = lax.axis_index("space"), lax.axis_index("tm")
    frames = o0.shape[0]
    for t, (who, rank) in enumerate(ranks(own_ref)):
        for d, src in enumerate((s0, s1, s2, s3)):

            @pl.when(who == (here ^ d))
            def _(src=src, t=t, rank=rank):
                for e, out in enumerate((o0, o1, o2, o3)):
                    for f in range(frames):
                        at = (((zed ^ e) * frames + f) * CAP + rank) * HALF
                        for h in range(HALF):
                            out[f, t, h] = src[at + h]


def join_body(a1, a3, out):
    out[0] = a1[...]
    out[1] = a3[...]


def by_group(rows, top, low):
    return jnp.where(rows < GSZ, top, low)


def own_channels(ref, slot):
    count = ref.shape[1]
    k = lax.broadcasted_iota(jnp.int32, (WIDE, count), 0)
    c = lax.broadcasted_iota(jnp.int32, (WIDE, count), 1)
    wanted = (k >> 4) * (count // HALF) + slot * GSZ + (k & (GSZ - 1))
    return jnp.sum(jnp.where(c == wanted, ref[...], 0.0), axis=1, keepdims=True)


def act_body(gain_ref, shift_ref, q0, q1, q2, q3, xh_ref, ds_ref, sh_ref, inv_ref):
    here, zed = lax.axis_index("space"), lax.axis_index("tm")
    local, tiles = q0.shape[:2]
    frames = xh_ref.shape[0]
    shape = (WIDE, LANES)
    rows = lax.broadcasted_iota(jnp.int32, shape, 0)
    lane = lax.broadcasted_iota(jnp.int32, shape, 1)
    count = float(frames * tiles * LANES * GSZ)
    acc = jnp.zeros(shape, F32)
    for e, q in enumerate((q0, q1, q2, q3)):
        for f in range(local):
            for t in range(tiles):
                x = q[f, here ^ t].astype(F32).reshape(shape)
                xh_ref[(zed ^ e) * local + f, t] = x
                acc = acc + x
    mean = by_group(rows, jnp.sum(acc[:GSZ]), jnp.sum(acc[GSZ:])) / count

    def spread_of(f, acc):
        for t in range(tiles):
            c = xh_ref[f, t] - mean
            acc = acc + c * c
        return acc

    acc = lax.fori_loop(0, frames, spread_of, jnp.zeros(shape, F32))
    var = by_group(rows, jnp.sum(acc[:GSZ]), jnp.sum(acc[GSZ:])) / count
    inv = lax.rsqrt(var + EPS)
    gain, shift = gain_ref[...], shift_ref[...]
    inv_ref[...] = inv
    col, row = lane & (TW - 1), lane >> 4

    def emit(f, carry):
        for t in range(tiles):
            normed = (xh_ref[f, t] - mean) * inv
            act = normed * gain + shift
            sig = jax.nn.sigmoid(act)
            hid = (act * sig).astype(BF16).astype(F32)
            xh_ref[f, t] = normed
            ds_ref[f, t] = sig * (1.0 + act * (1.0 - sig))
            left = jnp.where(col >= 1, pltpu.roll(hid, 1, 1), 0.0)
            right = jnp.where(col <= TW - 2, pltpu.roll(hid, LANES - 1, 1), 0.0)
            for kx, part in enumerate((left, hid, right)):
                up = jnp.where(row >= 1, pltpu.roll(part, TW, 1), 0.0)
                down = jnp.where(row <= TH - 2, pltpu.roll(part, LANES - TW, 1), 0.0)
                for ky, tap in enumerate((up, part, down)):
                    tap = tap.astype(BF16)
                    base = (ky * 3 + kx) * GSZ
                    for h in range(HALF):
                        sh_ref[f + 2, h, base : base + GSZ, t * LANES : (t + 1) * LANES] = tap[
                            h * GSZ : (h + 1) * GSZ
                        ]
        return carry

    lax.fori_loop(0, frames, emit, 0)
    sh_ref[0] = sh_ref[2]
    sh_ref[1] = sh_ref[2]


def place(gv, row, own, two, odd):
    zed = lax.axis_index("tm")
    local, cells = two.shape[0], two.shape[2]
    steps = cells // GSZ
    rows = slice(row, row + cells)
    for f in range(local):
        for o in range(2):
            lanes = slice(o * LANES, (o + 1) * LANES)
            if len(own.shape) == 3:
                at = own.shape[0] - (local * 2 - f * 2 - o) * steps
                gv[zed * local + f, rows, lanes] = own[at : at + steps].reshape(cells, LANES)
            else:
                gv[zed * local + f, rows, lanes] = own[f, o]
            gv[(zed ^ 2) * local + f, rows, lanes] = two[f, o]
            for e in (1, 3):
                gv[(zed ^ e) * local + f, rows, lanes] = odd[e // 2, f, o]
    frames = local * NZ
    for f in range(frames, frames + 2):
        gv[f, rows] = jnp.zeros((cells, gv.shape[2]), BF16)


def dot_nt(a, b):
    return lax.dot_general(a, b, (((1,), (1,)), ((), ())), preferred_element_type=F32)


def unshift(p, col, row):
    out = None
    for ky in range(3):
        part = [p[(ky * 3 + kx) * WIDE : (ky * 3 + kx + 1) * WIDE] for kx in range(3)]
        r = part[1]
        r = r + jnp.where(col <= TW - 2, pltpu.roll(part[0], LANES - 1, 1), 0.0)
        r = r + jnp.where(col >= 1, pltpu.roll(part[2], 1, 1), 0.0)
        if ky == 0:
            r = jnp.where(row <= TH - 2, pltpu.roll(r, LANES - TW, 1), 0.0)
        if ky == 2:
            r = jnp.where(row >= 1, pltpu.roll(r, TW, 1), 0.0)
        out = r if out is None else out + r
    return out


def hidden_grads(wv, gv, row, tiles, dh, res):
    shape = (WIDE, LANES)
    lane = lax.broadcasted_iota(jnp.int32, shape, 1)
    col, line = lane & (TW - 1), lane >> 4
    outs_ch = gv.shape[2]
    wide = 9 * WIDE
    frames = gv.shape[0] - 2
    step = 4 // tiles
    rows = slice(row, row + tiles * LANES)

    def grads_at(f, n=step):
        return gv[pl.ds(f, n), rows].reshape(n * tiles * LANES, outs_ch)

    def group(f, first):
        beside = jnp.concatenate([grads_at(f), grads_at(f + 1), grads_at(f + 2)], axis=1)
        total = dot_nt(wv[...].reshape(-1, 3 * outs_ch), beside)
        extra = None
        if first:
            now, then = grads_at(0, 1), grads_at(1, 1)
            late = wv[:9].reshape(wide, 3 * outs_ch)[:, outs_ch:]
            extra = dot_nt(late, jnp.concatenate([now, now], axis=1))
            extra = extra + dot_nt(late[:, outs_ch:], then)
        for n in range(step):
            for t in range(tiles):
                at = (n * tiles + t) * LANES
                p = total[:wide, at : at + LANES]
                if first and n == 0:
                    p = p + extra[:, t * LANES : (t + 1) * LANES]
                dh[f + n, t] = unshift(p, col, line)
                res[f + n, t] = total[wide : wide + GSZ, at : at + LANES]

    group(0, True)

    def later(n, carry):
        group(n * step, False)
        return carry

    lax.fori_loop(1, frames // step, later, 0)


def grad_near_body(wo, wp, g, a2, a13, r1, c2, c13, wv, gv, dh, res):
    zed, clip, here = lax.axis_index("tm"), lax.axis_index("dp"), lax.axis_index("space")
    outs_ch = wo.shape[2]
    for kt in range(3):
        lanes = slice((2 - kt) * outs_ch, (3 - kt) * outs_ch)
        for k in range(9):
            wv[k, clip, :, lanes] = wo[9 * kt + k]
            wv[k, 1 - clip, :, lanes] = wp[9 * kt + k]
    first = (zed * NS + here) * GSZ
    kk = lax.broadcasted_iota(jnp.int32, (GSZ, 3 * outs_ch), 0)
    oo = lax.broadcasted_iota(jnp.int32, (GSZ, 3 * outs_ch), 1)
    wv[9, 0] = jnp.where(oo == kk + first, 1.0, 0.0).astype(BF16)
    wv[9, 1] = jnp.zeros((GSZ, 3 * outs_ch), BF16)
    place(gv, 0, g, a2, a13)
    place(gv, LANES, r1, c2, c13)
    hidden_grads(wv, gv, 0, 2, dh, res)


def grad_far_body(wv, r2, y2, y13, gv, dh, res):
    place(gv, 0, r2, y2, y13)
    hidden_grads(wv, gv, 0, 1, dh, res)


def grad_last_body(wv, gv2, d0, d2, d13, dh01, res01, dh2, res2, xh, ds, gain_ref, inv_ref, *rest):
    (o0, o1, o2, o3, gv), (dh3, res3, dact) = rest[:5], rest[5:]
    here, zed = lax.axis_index("space"), lax.axis_index("tm")
    frames, tiles = xh.shape[:2]
    local = frames // NZ
    gv[:, :LANES] = gv2[...]
    place(gv, LANES, d0, d2, d13)
    hidden_grads(wv, gv, LANES, 1, dh3, res3)
    shape = (WIDE, LANES)
    rows = lax.broadcasted_iota(jnp.int32, shape, 0)
    lane = lax.broadcasted_iota(jnp.int32, shape, 1)
    parts = ((dh01, res01, 0), (dh01, res01, 1), (dh2, res2, 0), (dh3, res3, 0))

    def sums_of(f, sums):
        dg, db = sums
        for t, (dh, _, at) in enumerate(parts):
            da = dh[f, at] * ds[f, t]
            dact[f, t] = da
            dg = dg + da * xh[f, t]
            db = db + da
        return dg, db

    zero = jnp.zeros(shape, F32)
    dg, db = lax.fori_loop(0, frames, sums_of, (zero, zero))
    dg = jnp.sum(dg, axis=1, keepdims=True)
    db = jnp.sum(db, axis=1, keepdims=True)
    gain = gain_ref[...]
    inv = inv_ref[...]
    count = float(frames * tiles * LANES * GSZ)
    gb, gg = gain[:, :1] * db, gain[:, :1] * dg
    m1 = by_group(rows, jnp.sum(gb[:GSZ]), jnp.sum(gb[GSZ:])) / count
    m2 = by_group(rows, jnp.sum(gg[:GSZ]), jnp.sum(gg[GSZ:])) / count
    outs = (o0, o1, o2, o3)
    for e, out in enumerate(outs):
        for f in range(local):
            frame = (zed ^ e) * local + f
            for t, (_, res, at) in enumerate(parts):
                y = inv * (dact[frame, t] * gain - m1 - xh[frame, t] * m2)
                base = (f * tiles + (here ^ t)) * HALF
                out[base] = (y[:GSZ] + res[frame, at]).astype(BF16)
                out[base + 1] = y[GSZ:].astype(BF16)
    rscale = 1.0 / math.sqrt(lax.axis_size("dp") * frames * tiles * LANES)
    spot = lane == zed * WIDE + rows
    line = lax.broadcasted_iota(jnp.int32, (GSZ, LANES), 0)
    block = jnp.zeros((GSZ, LANES), F32)
    at = 0
    for value in (dg, db):
        value = jnp.sum(jnp.where(spot, value * rscale, 0.0), axis=0, keepdims=True)
        for _ in range(3):
            part = value.astype(BF16).astype(F32)
            block = jnp.where(line == at, part, block)
            value = value - part
            at += 1
    for out in outs:
        out[local * tiles * HALF] = block.astype(BF16)


def dweight_body(flip, sh_ref, near, far, *rest):
    outs, acc = rest[:-1], rest[-1]
    half = lax.axis_index("dp") ^ flip
    frames = near.shape[0] - 2
    pair = near.shape[1]
    acc[...] = jnp.zeros_like(acc)

    def frames_pair(n, carry):
        at = [2 * n, 2 * n + 1]
        taps = [sh_ref[pl.ds(f, 3), half].reshape(acc.shape[0], 2 * pair) for f in at]
        rows = [part[f] for f in at for part in (near, far)]
        acc[...] += jnp.dot(
            jnp.concatenate(taps, axis=1),
            jnp.concatenate(rows, axis=0),
            preferred_element_type=F32,
        )
        return carry

    lax.fori_loop(0, frames // 2, frames_pair, 0)
    rscale = 1.0 / math.sqrt(lax.axis_size("dp") * frames * 2 * pair)
    total = (acc[...] * rscale).reshape(-1, GSZ, acc.shape[1])
    start = 0
    for out in outs:
        out[...] = total[start : start + out.shape[0]]
        start += out.shape[0]


def expand_body(own_hbm, p0, p1, p2, p3, o0, o1, o2, o3, sums, own_ref, sem):
    copy = pltpu.make_async_copy(own_hbm, own_ref, sem)
    copy.start()
    here, zed = lax.axis_index("space"), lax.axis_index("tm")
    tiles = own_hbm.shape[0]
    local = (p0.shape[0] - 1) // tiles // HALF
    parts, outs = (p0, p1, p2, p3), (o0, o1, o2, o3)
    for out in outs:
        out[...] = jnp.zeros_like(out)
    block = jnp.zeros((GSZ, LANES), F32)
    for part in parts:
        block = block + part[local * tiles * HALF].astype(F32)
    sums[0:1] = block[0:1] + block[1:2] + block[2:3]
    sums[1:2] = block[3:4] + block[4:5] + block[5:6]
    sums[2:8] = jnp.zeros((6, LANES), F32)
    copy.wait()
    for t, (who, rank) in enumerate(ranks(own_ref)):
        for d, out in enumerate(outs):

            @pl.when(who == (here ^ d))
            def _(out=out, t=t, rank=rank):
                for e, part in enumerate(parts):
                    for f in range(local):
                        at = (((zed ^ e) * local + f) * CAP + rank) * HALF
                        base = (f * tiles + t) * HALF
                        for h in range(HALF):
                            out[at + h] = part[base + h]


def mix_body(mine, peer, out):
    out[...] = mine[...] + peer[...]


def final_body(*refs):
    parts, sums, (keep, got1, got2) = refs[0:4], refs[4:8], refs[8:11]
    (out_hbm, dw_hbm, dg_ref, db_ref), (buf, out_ref, dw_ref, sem) = refs[11:15], refs[15:]
    here = lax.axis_index("space")
    frames, cap = out_ref.shape[:2]
    first = got1.shape[0]
    dw_ref[:first] = keep[:first] + got1[...]
    dw_ref[first:] = keep[first:] + got2[...]
    copies = [pltpu.make_async_copy(dw_ref, dw_hbm, sem.at[frames * cap])]
    copies[0].start()
    for f in range(frames):
        for c in range(cap):
            spot = buf.at[f * cap + c]
            for d, part in enumerate(parts):
                for z in range(NZ):
                    for h in range(HALF):
                        at = ((z * frames + f) * cap + c) * HALF + h
                        spot[h * NZ * NS + z * NS + (here ^ d)] = part[at]
            out_ref[f, c] = spot[...].reshape(-1, LANES).T
            copy = pltpu.make_async_copy(out_ref.at[f, c], out_hbm.at[f, c], sem.at[f * cap + c])
            copy.start()
            copies.append(copy)
    chans = dg_ref.shape[1]
    lane = lax.broadcasted_iota(jnp.int32, (LANES, chans), 0)
    goal = lax.broadcasted_iota(jnp.int32, (LANES, chans), 1)
    source = ((goal >> 6) & 3) * WIDE + (goal >> 8) * GSZ + (goal & (GSZ - 1))
    sort = jnp.where(lane == source, 1.0, 0.0).astype(BF16)
    values = jnp.concatenate([part[...] for part in sums], axis=0)
    pieces = []
    for _ in range(3):
        pieces.append(values.astype(BF16))
        values = values - pieces[-1].astype(F32)
    moved = jnp.dot(jnp.concatenate(pieces, axis=0), sort, preferred_element_type=F32)
    count = values.shape[0]
    moved = moved[:count] + moved[count : 2 * count] + moved[2 * count :]
    owner = (lax.broadcasted_iota(jnp.int32, (8, chans), 1) >> 4) & 3
    total = jnp.zeros((8, chans), F32)
    for d in range(NS):
        total = jnp.where(owner == (here ^ d), moved[8 * d : 8 * d + 8], total)
    dg_ref[...] = total[0:1]
    db_ref[...] = total[1:2]
    for copy in copies:
        copy.wait()


def channel_plan(latents, owner, gamma, beta, weight, upstream):
    lat = latents[0]
    local, cap, cells, chans = lat.shape
    outs_ch = upstream.shape[4]
    tiles = owner.shape[1]
    frames = local * lax.axis_size("tm")
    taps = weight.shape[1]
    own = owner.reshape(tiles)
    slots = NZ * local * cap * HALF
    more = local * outs_ch // LANES * cells // GSZ
    own_w = weight.transpose(1, 0, 2)

    spread = [slots, slots + more, slots + more, slots]
    t0, t1, t2, t3, grads, gain, shift = kernel_step(
        prep_body,
        [VMEM((count, GSZ, cells), BF16) for count in spread]
        + [
            VMEM((local, outs_ch // LANES, cells, LANES), BF16),
            VMEM((WIDE, LANES), F32),
            VMEM((WIDE, LANES), F32),
        ],
        [],
        [
            VMEM((HALF * NZ * NS, GSZ, cells), BF16),
            VMEM((local, 4 * cells, outs_ch), BF16),
            VMEM(lat.shape, BF16),
            VMEM((1, chans), F32),
            VMEM((1, chans), F32),
            pltpu.SemaphoreType.DMA((4,)),
        ],
        entry=(
            upstream.reshape(local, 4 * cells, outs_ch),
            lat,
            gamma.reshape(1, chans),
            beta.reshape(1, chans),
        ),
    )
    along = [swap(grads, "tm", e) for e in (1, 2, 3)]
    r2, r3, r1 = (swap(v, "space", d) for v, d in ((t2, 2), (t3, 3), (t1, 1)))
    peer_w = swap(own_w, "dp", 1)
    d0 = swap(r2, "space", 1)
    owner_scratch = [pltpu.SMEM((tiles,), jnp.int32), pltpu.SemaphoreType.DMA]
    picked = kernel_step(
        pick_body,
        [VMEM((local, tiles, HALF, GSZ, cells), BF16)] * NZ,
        [t0, r1, r2, r3],
        owner_scratch,
        entry=(own,),
    )
    seen = [picked[0]] + [swap(picked[e], "tm", e) for e in (1, 2, 3)]
    a1, a2, a3 = along
    a13 = kernel_step(join_body, VMEM((2,) + grads.shape, BF16), [a1, a3])
    y2, c2 = swap(a2, "space", 2), swap(a2, "space", 1)
    y13, c13 = swap(a13, "space", 2), swap(a13, "space", 1)
    d2, d13 = swap(y2, "space", 1), swap(y13, "space", 1)
    normed, slope, shifts, inv = kernel_step(
        act_body,
        [
            VMEM((frames, tiles, WIDE, cells), F32),
            VMEM((frames, tiles, WIDE, cells), F32),
            VMEM((frames + 2, HALF, 9 * GSZ, tiles * cells), BF16),
            VMEM((WIDE, LANES), F32),
        ],
        [gain, shift] + seen,
    )

    def hidden_shapes(count):
        return [VMEM((frames, count, WIDE, cells), F32), VMEM((frames, count, GSZ, cells), F32)]

    taps_all, near, dh01, res01 = kernel_step(
        grad_near_body,
        [
            VMEM((10, HALF, GSZ, 3 * outs_ch), BF16),
            VMEM((frames + 2, 2 * cells, outs_ch), BF16),
        ]
        + hidden_shapes(2),
        [own_w, peer_w, grads, a2, a13, r1, c2, c13],
    )
    far2, dh2, res2 = kernel_step(
        grad_far_body,
        [VMEM((frames + 2, cells, outs_ch), BF16)] + hidden_shapes(1),
        [taps_all, r2, y2, y13],
    )
    shares = kernel_step(
        grad_last_body,
        [VMEM((local * tiles * HALF + 1, GSZ, cells), BF16)] * NZ
        + [VMEM((frames + 2, 2 * cells, outs_ch), BF16)],
        [taps_all, far2, d0, d2, d13, dh01, res01, dh2, res2, normed, slope, gain, inv],
        hidden_shapes(1) + [VMEM((frames, tiles, WIDE, cells), F32)],
    )
    far = shares[4]
    back = [shares[0]] + [swap(shares[e], "tm", e) for e in (1, 2, 3)]

    def dweight_half(flip, *parts):
        return kernel_step(
            lambda *refs: dweight_body(flip, *refs),
            [VMEM((part, GSZ, outs_ch), F32) for part in parts],
            [shifts, near, far],
            [VMEM((taps * GSZ, outs_ch), F32)],
        )

    send1, send2 = dweight_half(1, FIRST_TAPS, taps - FIRST_TAPS)
    got1, got2 = swap(send1, "dp", 1), swap(send2, "dp", 1)
    *spots, sums = kernel_step(
        expand_body,
        [VMEM((slots, GSZ, cells), BF16)] * NS + [VMEM((8, LANES), F32)],
        back,
        owner_scratch,
        entry=(own,),
    )
    home = [spots[0]] + [swap(spots[d], "space", d) for d in (1, 2, 3)]
    (keep,) = dweight_half(0, taps)
    mixed = kernel_step(mix_body, VMEM((8, LANES), F32), [sums, swap(sums, "dp", 1)])
    mixes = [mixed] + [swap(mixed, "space", d) for d in (1, 2, 3)]
    dlatent, dweight, dgamma, dbeta = kernel_step(
        final_body,
        [
            pltpu.HBM((local, cap, cells, chans), BF16),
            pltpu.HBM((taps, GSZ, outs_ch), F32),
            jax.ShapeDtypeStruct((1, chans), F32),
            jax.ShapeDtypeStruct((1, chans), F32),
        ],
        home + mixes + [keep, got1, got2],
        [
            VMEM((local * cap, HALF * NZ * NS, GSZ, cells), BF16),
            VMEM((local, cap, cells, chans), BF16),
            VMEM((taps, GSZ, outs_ch), F32),
            pltpu.SemaphoreType.DMA((local * cap + 1,)),
        ],
    )
    return (dlatent[None], dweight.transpose(1, 0, 2), dgamma.reshape(chans), dbeta.reshape(chans))


def fits_plan(sizes, latents, weight, upstream):
    return (
        sizes == [HALF, NZ, NS]
        and weight.shape[0] == GSZ
        and latents.shape[4] == GROUPS * GSZ
        and latents.shape[0] == 1
        and latents.shape[2] == CAP
        and upstream.shape[2] == 1
        and latents.shape[3] == LANES
    )


def body(latents, owner, gamma, beta, weight, upstream):
    args = (latents, owner, gamma, beta, weight, upstream)
    sizes = [lax.axis_size(a) for a in ("dp", "tm", "space")]
    if not fits_plan(sizes, latents, weight, upstream):
        return shards(*args)
    return channel_plan(*args)


def solution(mesh):
    return jax.shard_map(
        body,
        mesh=mesh,
        in_specs=(
            P("dp", "tm", "space", None, None),
            P("dp", None, None),
            P(),
            P(),
            P(("dp", "tm", "space"), None, None),
            P("dp", "tm", "space", None, None),
        ),
        out_specs=(
            P("dp", "tm", "space", None, None),
            P(("dp", "tm", "space"), None, None),
            P(),
            P(),
        ),
        check_vma=False,
    )
```

```python
import math

import jax
import jax.numpy as jnp
from jax import lax
from jax.experimental import pallas as pl
from jax.experimental.pallas import tpu as pltpu
from jax.sharding import PartitionSpec as P


GROUPS = 32
TH = 8
TW = 16


EPS = 1e-06


def shifted(value, axis, steps):
    count = lax.axis_size(axis)
    initial, last = (max(0, -steps), min(count, count - steps))
    return lax.ppermute(value, axis, [(source, source + steps) for source in range(initial, last)])


def tap_list():
    return [(kt, ky, kx) for kt in range(3) for ky in range(3) for kx in range(3)]


def conv_grads(hidden, grads, weight, rscale):
    frames, count, cells, chans = hidden.shape
    outs_ch = grads.shape[3]
    first_dev = lax.axis_index("tm") == 0
    cache = shifted(hidden, "tm", 1)
    repeat = jnp.concatenate([hidden[:1], hidden[:1]], axis=0)
    cache = jnp.where(first_dev, repeat, cache)
    extended = jnp.concatenate([cache, hidden], axis=0).reshape(frames + 2, count, TH, TW, chans)
    padded = jnp.pad(extended, ((0, 0), (0, 0), (1, 1), (1, 1), (0, 0)))
    rows = grads.reshape(frames * count * cells, outs_ch)
    span = lax.axis_size(("dp", "tm", "space")) * weight.shape[0]
    terms = []
    for kt, ky, kx in tap_list():
        tap = padded[kt : kt + frames, :, ky : ky + TH, kx : kx + TW].reshape(
            frames * count * cells, span
        )
        terms.append(
            lax.dot_general(tap, rows, (((0,), (0,)), ((), ())), preferred_element_type=jnp.float32)
        )
    dweight = lax.psum_scatter(
        jnp.stack(terms, axis=1) * rscale, ("dp", "tm", "space"), scatter_dimension=0, tiled=True
    )
    piece = lax.all_gather(weight, ("dp", "tm", "space"), axis=0, tiled=True)
    span = piece.shape[0]
    total = jnp.zeros((frames + 2, count, TH + 2, TW + 2, span), jnp.float32)
    for index, (kt, ky, kx) in enumerate(tap_list()):
        back = lax.dot_general(
            rows, piece[:, index, :], (((1,), (1,)), ((), ())), preferred_element_type=jnp.float32
        )
        total = total.at[kt : kt + frames, :, ky : ky + TH, kx : kx + TW].add(
            back.reshape(frames, count, TH, TW, span)
        )
    dextended = total[:, :, 1 : TH + 1, 1 : TW + 1].reshape(frames + 2, count, cells, span)
    carried = shifted(dextended[:2].astype(jnp.bfloat16), "tm", -1).astype(jnp.float32)
    own_part = dextended[2:]
    own_part = own_part.at[frames - 2 :].add(carried)
    own_part = own_part.at[0].add(jnp.where(first_dev, dextended[0] + dextended[1], 0.0))
    return (own_part, dweight)


def shards(latents, owner, gamma, beta, weight, upstream):
    blocks = latents[0]
    frames, cap, cells, chans = blocks.shape
    spaces = lax.axis_size("space")
    here = lax.axis_index("space")
    per_dev = upstream.shape[2]
    outs_ch = upstream.shape[4]
    tile_ids = owner[0, :, 0]
    tiles = tile_ids.shape[0]
    width = chans // GROUPS
    hot = (tile_ids[:, None] == jnp.arange(spaces, dtype=jnp.int32)[None, :]).astype(jnp.int32)
    rank = jnp.sum((jnp.cumsum(hot, axis=0) - hot) * hot, axis=1)
    slot = tile_ids * cap + rank
    holds = slot[None, :] == (here * cap + jnp.arange(cap, dtype=jnp.int32))[:, None]
    live = jnp.any(holds, axis=1).astype(jnp.float32)
    tile_of = jnp.sum(holds.astype(jnp.int32) * jnp.arange(tiles, dtype=jnp.int32)[None, :], axis=1)
    frames_all = frames * lax.axis_size("tm")
    count = float(frames_all * tiles * cells * width)
    rscale = 1.0 / math.sqrt(lax.axis_size("dp") * frames_all * tiles * cells)
    values = blocks.astype(jnp.float32).reshape(frames, cap, cells, GROUPS, width)
    live_mask = live[None, :, None, None, None]
    total = lax.psum(jnp.sum(values * live_mask, axis=(0, 1, 2, 4)), ("tm", "space"))
    mean = total / count
    centred = values - mean[:, None]
    spread = lax.psum(jnp.sum(centred * centred * live_mask, axis=(0, 1, 2, 4)), ("tm", "space"))
    var = spread / count
    inverse = lax.rsqrt(var + EPS)
    normed = (centred * inverse[:, None]).reshape(frames, cap, cells, chans)
    act = normed * gamma + beta
    sig = jax.nn.sigmoid(act)
    hidden = (act * sig).astype(jnp.bfloat16)
    ups = upstream[0].astype(jnp.float32).reshape(frames, per_dev, TH, 2, TW, 2, outs_ch)
    pooled = jnp.sum(ups, axis=(3, 5)).reshape(frames, per_dev, cells, outs_ch).astype(jnp.bfloat16)
    all_pooled = lax.all_gather(pooled, "space", axis=1, tiled=True)
    live_slot = live[None, :, None, None] > 0.5
    grads = jnp.where(live_slot, all_pooled[:, tile_of], jnp.zeros((), jnp.bfloat16))
    dhidden, dweight = conv_grads(hidden, grads, weight, rscale)
    dact = dhidden * (sig * (1.0 + act * (1.0 - sig))) * live[None, :, None, None]
    dgamma, dbeta = lax.psum(
        (jnp.sum(dact * normed, axis=(0, 1, 2)) * rscale, jnp.sum(dact, axis=(0, 1, 2)) * rscale),
        ("dp", "tm", "space"),
    )
    dnorm = (dact * gamma).reshape(frames, cap, cells, GROUPS, width)
    ngroup = normed.reshape(frames, cap, cells, GROUPS, width)
    first_m, second_m = lax.psum(
        (jnp.sum(dnorm, axis=(0, 1, 2, 4)), jnp.sum(dnorm * ngroup, axis=(0, 1, 2, 4))),
        ("tm", "space"),
    )
    dvalues = inverse[:, None] * (
        dnorm - (first_m / count)[:, None] - ngroup * (second_m / count)[:, None]
    )
    dfull = dvalues.reshape(frames, cap, cells, chans)
    resid = jnp.pad(grads.astype(jnp.float32), ((0, 0), (0, 0), (0, 0), (0, chans - outs_ch)))
    dlatent = ((dfull + resid) * live[None, :, None, None]).astype(jnp.bfloat16)
    return (dlatent[None], dweight, dgamma, dbeta)


LANES = 128
HALF = 2
NZ = 4
NS = 4
CAP = 2
GSZ = 16
FIRST_TAPS = 18
WIDE = HALF * GSZ

F32 = jnp.float32
BF16 = jnp.bfloat16
VMEM = pltpu.VMEM


def swap(value, axis, mask):
    count = lax.axis_size(axis)
    return lax.ppermute(value, axis, [(i, i ^ mask) for i in range(count)])


def kernel_step(body, outs, ins, scratch=(), entry=(), scalars=(), limit=24):
    held = [pltpu.with_memory_space_constraint(a, VMEM) for a in ins]
    small = [pltpu.with_memory_space_constraint(a, pltpu.SMEM) for a in scalars]
    return pl.pallas_call(
        body,
        out_shape=outs,
        in_specs=[pl.BlockSpec(memory_space=pltpu.SMEM)] * len(small)
        + [pl.BlockSpec(memory_space=pltpu.HBM)] * len(entry)
        + [pl.BlockSpec(memory_space=VMEM)] * len(held),
        out_specs=jax.tree.map(space_of, outs),
        scratch_shapes=list(scratch),
        compiler_params=pltpu.CompilerParams(vmem_limit_bytes=limit * 1024 * 1024),
    )(*small, *[pltpu.with_memory_space_constraint(a, pltpu.HBM) for a in entry], *held)


def space_of(out):
    return pl.BlockSpec(memory_space=getattr(out, "memory_space", VMEM))


def prep_body(up_hbm, lat_hbm, gamma_hbm, beta_hbm, own_hbm, *rest):
    (o0, o1, o2, o3, g_ref, gain, shift, spots) = rest[:8]
    buf, up_ref, lat_ref, gamma_ref, beta_ref, own_ref, sem = rest[8:]
    wanted = ((up_hbm, up_ref), (lat_hbm, lat_ref), (gamma_hbm, gamma_ref))
    wanted = wanted + ((beta_hbm, beta_ref), (own_hbm, own_ref))
    copies = [
        pltpu.make_async_copy(src, dst, sem.at[n]) for n, (src, dst) in enumerate(wanted)
    ]
    for copy in copies:
        copy.start()
    here = lax.axis_index("space")
    frames, cap, cells = lat_ref.shape[:3]
    fine = up_ref.shape[1]
    q = lax.broadcasted_iota(jnp.int32, (cells, fine), 0)
    p = lax.broadcasted_iota(jnp.int32, (cells, fine), 1)
    coarse = (p >> 6) * TW + ((p & (2 * TW - 1)) >> 1)
    mix = jnp.where(coarse == q, 1.0, 0.0).astype(BF16)
    slots = NZ * frames * cap * HALF
    copies[0].wait()
    for f in range(frames):
        pooled = jnp.dot(mix, up_ref[f], preferred_element_type=F32).astype(BF16)
        for o in range(pooled.shape[1] // LANES):
            part = pooled[:, o * LANES : (o + 1) * LANES]
            g_ref[f, o] = part
            rows = cells // GSZ
            base = slots + (f * 2 + o) * rows
            o1[base : base + rows] = part.reshape(rows, GSZ, LANES)
            o2[base : base + rows] = part.reshape(rows, GSZ, LANES)
    copies[1].wait()
    for f in range(frames):
        for c in range(cap):
            buf[...] = lat_ref[f, c].T.reshape(buf.shape)
            for d, out in enumerate((o0, o1, o2, o3)):
                for z in range(NZ):
                    for h in range(HALF):
                        at = ((z * frames + f) * cap + c) * HALF + h
                        out[at] = buf[h * NZ * NS + z * NS + (here ^ d)]
    copies[2].wait()
    copies[3].wait()
    slot = lax.axis_index("tm") * NS + here
    gain[...] = jnp.broadcast_to(own_channels(gamma_ref, slot), gain.shape)
    shift[...] = jnp.broadcast_to(own_channels(beta_ref, slot), shift.shape)
    copies[4].wait()
    for t, (who, rank) in enumerate(ranks(own_ref)):
        spots[2 * t] = who
        spots[2 * t + 1] = rank


def ranks(own_ref):
    out = []
    for t in range(own_ref.shape[0]):
        rank = jnp.int32(0)
        for before in range(t):
            rank = rank + jnp.where(own_ref[before] == own_ref[t], 1, 0)
        out.append((own_ref[t], rank))
    return out


def pick_body(spots, s0, s1, s2, s3, o0, o1, o2, o3):
    here, zed = lax.axis_index("space"), lax.axis_index("tm")
    frames = o0.shape[0]
    for t in range(o0.shape[1]):
        who, rank = spots[2 * t], spots[2 * t + 1]
        for d, src in enumerate((s0, s1, s2, s3)):

            @pl.when(who == (here ^ d))
            def _(src=src, t=t, rank=rank):
                for e, out in enumerate((o0, o1, o2, o3)):
                    for f in range(frames):
                        at = (((zed ^ e) * frames + f) * CAP + rank) * HALF
                        for h in range(HALF):
                            out[f, t, h] = src[at + h]


def join_body(a1, a3, out):
    out[0] = a1[...]
    out[1] = a3[...]


def by_group(rows, top, low):
    return jnp.where(rows < GSZ, top, low)


def own_channels(ref, slot):
    count = ref.shape[1]
    k = lax.broadcasted_iota(jnp.int32, (WIDE, count), 0)
    c = lax.broadcasted_iota(jnp.int32, (WIDE, count), 1)
    wanted = (k >> 4) * (count // HALF) + slot * GSZ + (k & (GSZ - 1))
    return jnp.sum(jnp.where(c == wanted, ref[...], 0.0), axis=1, keepdims=True)


def act_body(gain_ref, shift_ref, q0, q1, q2, q3, xh_ref, ds_ref, sh_ref, inv_ref):
    here, zed = lax.axis_index("space"), lax.axis_index("tm")
    local, tiles = q0.shape[:2]
    frames = xh_ref.shape[0]
    shape = (WIDE, LANES)
    rows = lax.broadcasted_iota(jnp.int32, shape, 0)
    lane = lax.broadcasted_iota(jnp.int32, shape, 1)
    count = float(frames * tiles * LANES * GSZ)
    acc = jnp.zeros(shape, F32)
    for e, q in enumerate((q0, q1, q2, q3)):
        for f in range(local):
            for t in range(tiles):
                x = q[f, here ^ t].astype(F32).reshape(shape)
                xh_ref[(zed ^ e) * local + f, t] = x
                acc = acc + x
    mean = by_group(rows, jnp.sum(acc[:GSZ]), jnp.sum(acc[GSZ:])) / count

    def spread_of(f, acc):
        for t in range(tiles):
            c = xh_ref[f, t] - mean
            acc = acc + c * c
        return acc

    acc = lax.fori_loop(0, frames, spread_of, jnp.zeros(shape, F32))
    var = by_group(rows, jnp.sum(acc[:GSZ]), jnp.sum(acc[GSZ:])) / count
    inv = lax.rsqrt(var + EPS)
    gain, shift = gain_ref[...], shift_ref[...]
    inv_ref[...] = inv
    col, row = lane & (TW - 1), lane >> 4

    def emit(f, carry):
        for t in range(tiles):
            normed = (xh_ref[f, t] - mean) * inv
            act = normed * gain + shift
            sig = jax.nn.sigmoid(act)
            hid = (act * sig).astype(BF16).astype(F32)
            xh_ref[f, t] = normed
            ds_ref[f, t] = sig * (1.0 + act * (1.0 - sig))
            left = jnp.where(col >= 1, pltpu.roll(hid, 1, 1), 0.0)
            right = jnp.where(col <= TW - 2, pltpu.roll(hid, LANES - 1, 1), 0.0)
            for kx, part in enumerate((left, hid, right)):
                up = jnp.where(row >= 1, pltpu.roll(part, TW, 1), 0.0)
                down = jnp.where(row <= TH - 2, pltpu.roll(part, LANES - TW, 1), 0.0)
                for ky, tap in enumerate((up, part, down)):
                    tap = tap.astype(BF16)
                    base = (ky * 3 + kx) * GSZ
                    for h in range(HALF):
                        sh_ref[f + 2, h, base : base + GSZ, t * LANES : (t + 1) * LANES] = tap[
                            h * GSZ : (h + 1) * GSZ
                        ]
        return carry

    lax.fori_loop(0, frames, emit, 0)
    sh_ref[0] = sh_ref[2]
    sh_ref[1] = sh_ref[2]


def place(gv, row, own, two, odd):
    zed = lax.axis_index("tm")
    local, cells = two.shape[0], two.shape[2]
    steps = cells // GSZ
    rows = slice(row, row + cells)
    for f in range(local):
        for o in range(2):
            lanes = slice(o * LANES, (o + 1) * LANES)
            if len(own.shape) == 3:
                at = own.shape[0] - (local * 2 - f * 2 - o) * steps
                gv[zed * local + f, rows, lanes] = own[at : at + steps].reshape(cells, LANES)
            else:
                gv[zed * local + f, rows, lanes] = own[f, o]
            gv[(zed ^ 2) * local + f, rows, lanes] = two[f, o]
            for e in (1, 3):
                gv[(zed ^ e) * local + f, rows, lanes] = odd[e // 2, f, o]
    frames = local * NZ
    for f in range(frames, frames + 2):
        gv[f, rows] = jnp.zeros((cells, gv.shape[2]), BF16)


def dot_nt(a, b):
    return lax.dot_general(a, b, (((1,), (1,)), ((), ())), preferred_element_type=F32)


def unshift(p, col, row):
    out = None
    for ky in range(3):
        part = [p[(ky * 3 + kx) * WIDE : (ky * 3 + kx + 1) * WIDE] for kx in range(3)]
        r = part[1]
        r = r + jnp.where(col <= TW - 2, pltpu.roll(part[0], LANES - 1, 1), 0.0)
        r = r + jnp.where(col >= 1, pltpu.roll(part[2], 1, 1), 0.0)
        if ky == 0:
            r = jnp.where(row <= TH - 2, pltpu.roll(r, LANES - TW, 1), 0.0)
        if ky == 2:
            r = jnp.where(row >= 1, pltpu.roll(r, TW, 1), 0.0)
        out = r if out is None else out + r
    return out


def hidden_grads(wv, gv, row, tiles, dh, res):
    shape = (WIDE, LANES)
    lane = lax.broadcasted_iota(jnp.int32, shape, 1)
    col, line = lane & (TW - 1), lane >> 4
    outs_ch = gv.shape[2]
    wide = 9 * WIDE
    frames = gv.shape[0] - 2
    step = 4 // tiles
    rows = slice(row, row + tiles * LANES)

    def grads_at(f, n=step):
        return gv[pl.ds(f, n), rows].reshape(n * tiles * LANES, outs_ch)

    def group(f, first):
        beside = jnp.concatenate([grads_at(f), grads_at(f + 1), grads_at(f + 2)], axis=1)
        total = dot_nt(wv[...].reshape(-1, 3 * outs_ch), beside)
        extra = None
        if first:
            now, then = grads_at(0, 1), grads_at(1, 1)
            late = wv[:9].reshape(wide, 3 * outs_ch)[:, outs_ch:]
            extra = dot_nt(late, jnp.concatenate([now, now], axis=1))
            extra = extra + dot_nt(late[:, outs_ch:], then)
        for n in range(step):
            for t in range(tiles):
                at = (n * tiles + t) * LANES
                p = total[:wide, at : at + LANES]
                if first and n == 0:
                    p = p + extra[:, t * LANES : (t + 1) * LANES]
                dh[f + n, t] = unshift(p, col, line)
                res[f + n, t] = total[wide : wide + GSZ, at : at + LANES]

    group(0, True)

    def later(n, carry):
        group(n * step, False)
        return carry

    lax.fori_loop(1, frames // step, later, 0)


def grad_near_body(wo, wp, g, a2, a13, r1, c2, c13, wv, gv, dh, res):
    zed, clip, here = lax.axis_index("tm"), lax.axis_index("dp"), lax.axis_index("space")
    outs_ch = wo.shape[2]
    for kt in range(3):
        lanes = slice((2 - kt) * outs_ch, (3 - kt) * outs_ch)
        for k in range(9):
            wv[k, clip, :, lanes] = wo[9 * kt + k]
            wv[k, 1 - clip, :, lanes] = wp[9 * kt + k]
    first = (zed * NS + here) * GSZ
    kk = lax.broadcasted_iota(jnp.int32, (GSZ, 3 * outs_ch), 0)
    oo = lax.broadcasted_iota(jnp.int32, (GSZ, 3 * outs_ch), 1)
    wv[9, 0] = jnp.where(oo == kk + first, 1.0, 0.0).astype(BF16)
    wv[9, 1] = jnp.zeros((GSZ, 3 * outs_ch), BF16)
    place(gv, 0, g, a2, a13)
    place(gv, LANES, r1, c2, c13)
    hidden_grads(wv, gv, 0, 2, dh, res)


def grad_far_body(wv, r2, y2, y13, gv, dh, res):
    place(gv, 0, r2, y2, y13)
    hidden_grads(wv, gv, 0, 1, dh, res)


def grad_last_body(wv, gv2, d0, d2, d13, dh01, res01, dh2, res2, xh, ds, gain_ref, inv_ref, *rest):
    (o0, o1, o2, o3, gv), (dh3, res3, dact) = rest[:5], rest[5:]
    here, zed = lax.axis_index("space"), lax.axis_index("tm")
    frames, tiles = xh.shape[:2]
    local = frames // NZ
    gv[:, :LANES] = gv2[...]
    place(gv, LANES, d0, d2, d13)
    hidden_grads(wv, gv, LANES, 1, dh3, res3)
    shape = (WIDE, LANES)
    rows = lax.broadcasted_iota(jnp.int32, shape, 0)
    lane = lax.broadcasted_iota(jnp.int32, shape, 1)
    parts = ((dh01, res01, 0), (dh01, res01, 1), (dh2, res2, 0), (dh3, res3, 0))

    def sums_of(f, sums):
        dg, db = sums
        for t, (dh, _, at) in enumerate(parts):
            da = dh[f, at] * ds[f, t]
            dact[f, t] = da
            dg = dg + da * xh[f, t]
            db = db + da
        return dg, db

    zero = jnp.zeros(shape, F32)
    dg, db = lax.fori_loop(0, frames, sums_of, (zero, zero))
    dg = jnp.sum(dg, axis=1, keepdims=True)
    db = jnp.sum(db, axis=1, keepdims=True)
    gain = gain_ref[...]
    inv = inv_ref[...]
    count = float(frames * tiles * LANES * GSZ)
    gb, gg = gain[:, :1] * db, gain[:, :1] * dg
    m1 = by_group(rows, jnp.sum(gb[:GSZ]), jnp.sum(gb[GSZ:])) / count
    m2 = by_group(rows, jnp.sum(gg[:GSZ]), jnp.sum(gg[GSZ:])) / count
    outs = (o0, o1, o2, o3)
    for e, out in enumerate(outs):
        for f in range(local):
            frame = (zed ^ e) * local + f
            for t, (_, res, at) in enumerate(parts):
                y = inv * (dact[frame, t] * gain - m1 - xh[frame, t] * m2)
                base = (f * tiles + (here ^ t)) * HALF
                out[base] = (y[:GSZ] + res[frame, at]).astype(BF16)
                out[base + 1] = y[GSZ:].astype(BF16)
    rscale = 1.0 / math.sqrt(lax.axis_size("dp") * frames * tiles * LANES)
    spot = lane == zed * WIDE + rows
    line = lax.broadcasted_iota(jnp.int32, (GSZ, LANES), 0)
    block = jnp.zeros((GSZ, LANES), F32)
    at = 0
    for value in (dg, db):
        value = jnp.sum(jnp.where(spot, value * rscale, 0.0), axis=0, keepdims=True)
        for _ in range(3):
            part = value.astype(BF16).astype(F32)
            block = jnp.where(line == at, part, block)
            value = value - part
            at += 1
    for out in outs:
        out[local * tiles * HALF] = block.astype(BF16)


def dweight_body(flip, sh_ref, near, far, *rest):
    outs, acc = rest[:-1], rest[-1]
    half = lax.axis_index("dp") ^ flip
    frames = near.shape[0] - 2
    pair = near.shape[1]
    acc[...] = jnp.zeros_like(acc)

    def frames_pair(n, carry):
        at = [2 * n, 2 * n + 1]
        taps = [sh_ref[pl.ds(f, 3), half].reshape(acc.shape[0], 2 * pair) for f in at]
        rows = [part[f] for f in at for part in (near, far)]
        acc[...] += jnp.dot(
            jnp.concatenate(taps, axis=1),
            jnp.concatenate(rows, axis=0),
            preferred_element_type=F32,
        )
        return carry

    lax.fori_loop(0, frames // 2, frames_pair, 0)
    rscale = 1.0 / math.sqrt(lax.axis_size("dp") * frames * 2 * pair)
    total = (acc[...] * rscale).reshape(-1, GSZ, acc.shape[1])
    start = 0
    for out in outs:
        out[...] = total[start : start + out.shape[0]]
        start += out.shape[0]


def expand_body(spots, p0, p1, p2, p3, o0, o1, o2, o3, sums):
    here, zed = lax.axis_index("space"), lax.axis_index("tm")
    tiles = spots.shape[0] // 2
    local = (p0.shape[0] - 1) // tiles // HALF
    parts, outs = (p0, p1, p2, p3), (o0, o1, o2, o3)
    for out in outs:
        out[...] = jnp.zeros_like(out)
    block = jnp.zeros((GSZ, LANES), F32)
    for part in parts:
        block = block + part[local * tiles * HALF].astype(F32)
    sums[0:1] = block[0:1] + block[1:2] + block[2:3]
    sums[1:2] = block[3:4] + block[4:5] + block[5:6]
    sums[2:8] = jnp.zeros((6, LANES), F32)
    for t in range(tiles):
        who, rank = spots[2 * t], spots[2 * t + 1]
        for d, out in enumerate(outs):

            @pl.when(who == (here ^ d))
            def _(out=out, t=t, rank=rank):
                for e, part in enumerate(parts):
                    for f in range(local):
                        at = (((zed ^ e) * local + f) * CAP + rank) * HALF
                        base = (f * tiles + t) * HALF
                        for h in range(HALF):
                            out[at + h] = part[base + h]


def mix_body(mine, peer, out):
    out[...] = mine[...] + peer[...]


def final_body(*refs):
    parts, sums, (keep, got1, got2) = refs[0:4], refs[4:8], refs[8:11]
    (out_hbm, dw_hbm, dg_ref, db_ref), (buf, out_ref, dw_ref, sem) = refs[11:15], refs[15:]
    here = lax.axis_index("space")
    frames, cap = out_ref.shape[:2]
    first = got1.shape[0]
    dw_ref[:first] = keep[:first] + got1[...]
    dw_ref[first:] = keep[first:] + got2[...]
    copies = [pltpu.make_async_copy(dw_ref, dw_hbm, sem.at[frames * cap])]
    copies[0].start()
    for f in range(frames):
        for c in range(cap):
            spot = buf.at[f * cap + c]
            for d, part in enumerate(parts):
                for z in range(NZ):
                    for h in range(HALF):
                        at = ((z * frames + f) * cap + c) * HALF + h
                        spot[h * NZ * NS + z * NS + (here ^ d)] = part[at]
            out_ref[f, c] = spot[...].reshape(-1, LANES).T
            copy = pltpu.make_async_copy(out_ref.at[f, c], out_hbm.at[f, c], sem.at[f * cap + c])
            copy.start()
            copies.append(copy)
    chans = dg_ref.shape[1]
    lane = lax.broadcasted_iota(jnp.int32, (LANES, chans), 0)
    goal = lax.broadcasted_iota(jnp.int32, (LANES, chans), 1)
    source = ((goal >> 6) & 3) * WIDE + (goal >> 8) * GSZ + (goal & (GSZ - 1))
    sort = jnp.where(lane == source, 1.0, 0.0).astype(BF16)
    values = jnp.concatenate([part[...] for part in sums], axis=0)
    pieces = []
    for _ in range(3):
        pieces.append(values.astype(BF16))
        values = values - pieces[-1].astype(F32)
    moved = jnp.dot(jnp.concatenate(pieces, axis=0), sort, preferred_element_type=F32)
    count = values.shape[0]
    moved = moved[:count] + moved[count : 2 * count] + moved[2 * count :]
    owner = (lax.broadcasted_iota(jnp.int32, (8, chans), 1) >> 4) & 3
    total = jnp.zeros((8, chans), F32)
    for d in range(NS):
        total = jnp.where(owner == (here ^ d), moved[8 * d : 8 * d + 8], total)
    dg_ref[...] = total[0:1]
    db_ref[...] = total[1:2]
    for copy in copies:
        copy.wait()


def channel_plan(latents, owner, gamma, beta, weight, upstream):
    lat = latents[0]
    local, cap, cells, chans = lat.shape
    outs_ch = upstream.shape[4]
    tiles = owner.shape[1]
    frames = local * lax.axis_size("tm")
    taps = weight.shape[1]
    own = owner.reshape(tiles)
    slots = NZ * local * cap * HALF
    more = local * outs_ch // LANES * cells // GSZ
    own_w = weight.transpose(1, 0, 2)

    spread = [slots, slots + more, slots + more, slots]
    t0, t1, t2, t3, grads, gain, shift, spot_table = kernel_step(
        prep_body,
        [VMEM((count, GSZ, cells), BF16) for count in spread]
        + [
            VMEM((local, outs_ch // LANES, cells, LANES), BF16),
            VMEM((WIDE, LANES), F32),
            VMEM((WIDE, LANES), F32),
            pltpu.SMEM((2 * tiles,), jnp.int32),
        ],
        [],
        [
            VMEM((HALF * NZ * NS, GSZ, cells), BF16),
            VMEM((local, 4 * cells, outs_ch), BF16),
            VMEM(lat.shape, BF16),
            VMEM((1, chans), F32),
            VMEM((1, chans), F32),
            pltpu.SMEM((tiles,), jnp.int32),
            pltpu.SemaphoreType.DMA((5,)),
        ],
        entry=(
            upstream.reshape(local, 4 * cells, outs_ch),
            lat,
            gamma.reshape(1, chans),
            beta.reshape(1, chans),
            own,
        ),
    )
    along = [swap(grads, "tm", e) for e in (1, 2, 3)]
    r2, r3, r1 = (swap(v, "space", d) for v, d in ((t2, 2), (t3, 3), (t1, 1)))
    peer_w = swap(own_w, "dp", 1)
    d0 = swap(r2, "space", 1)
    picked = kernel_step(
        pick_body,
        [VMEM((local, tiles, HALF, GSZ, cells), BF16)] * NZ,
        [t0, r1, r2, r3],
        scalars=(spot_table,),
    )
    seen = [picked[0]] + [swap(picked[e], "tm", e) for e in (1, 2, 3)]
    a1, a2, a3 = along
    a13 = kernel_step(join_body, VMEM((2,) + grads.shape, BF16), [a1, a3])
    y2, c2 = swap(a2, "space", 2), swap(a2, "space", 1)
    y13, c13 = swap(a13, "space", 2), swap(a13, "space", 1)
    d2, d13 = swap(y2, "space", 1), swap(y13, "space", 1)
    normed, slope, shifts, inv = kernel_step(
        act_body,
        [
            VMEM((frames, tiles, WIDE, cells), F32),
            VMEM((frames, tiles, WIDE, cells), F32),
            VMEM((frames + 2, HALF, 9 * GSZ, tiles * cells), BF16),
            VMEM((WIDE, LANES), F32),
        ],
        [gain, shift] + seen,
    )

    def hidden_shapes(count):
        return [VMEM((frames, count, WIDE, cells), F32), VMEM((frames, count, GSZ, cells), F32)]

    taps_all, near, dh01, res01 = kernel_step(
        grad_near_body,
        [
            VMEM((10, HALF, GSZ, 3 * outs_ch), BF16),
            VMEM((frames + 2, 2 * cells, outs_ch), BF16),
        ]
        + hidden_shapes(2),
        [own_w, peer_w, grads, a2, a13, r1, c2, c13],
    )
    far2, dh2, res2 = kernel_step(
        grad_far_body,
        [VMEM((frames + 2, cells, outs_ch), BF16)] + hidden_shapes(1),
        [taps_all, r2, y2, y13],
    )
    shares = kernel_step(
        grad_last_body,
        [VMEM((local * tiles * HALF + 1, GSZ, cells), BF16)] * NZ
        + [VMEM((frames + 2, 2 * cells, outs_ch), BF16)],
        [taps_all, far2, d0, d2, d13, dh01, res01, dh2, res2, normed, slope, gain, inv],
        hidden_shapes(1) + [VMEM((frames, tiles, WIDE, cells), F32)],
    )
    far = shares[4]
    back = [shares[0]] + [swap(shares[e], "tm", e) for e in (1, 2, 3)]

    def dweight_half(flip, *parts):
        return kernel_step(
            lambda *refs: dweight_body(flip, *refs),
            [VMEM((part, GSZ, outs_ch), F32) for part in parts],
            [shifts, near, far],
            [VMEM((taps * GSZ, outs_ch), F32)],
        )

    send1, send2 = dweight_half(1, FIRST_TAPS, taps - FIRST_TAPS)
    got1, got2 = swap(send1, "dp", 1), swap(send2, "dp", 1)
    *spots, sums = kernel_step(
        expand_body,
        [VMEM((slots, GSZ, cells), BF16)] * NS + [VMEM((8, LANES), F32)],
        back,
        scalars=(spot_table,),
    )
    home = [spots[0]] + [swap(spots[d], "space", d) for d in (1, 2, 3)]
    (keep,) = dweight_half(0, taps)
    mixed = kernel_step(mix_body, VMEM((8, LANES), F32), [sums, swap(sums, "dp", 1)])
    mixes = [mixed] + [swap(mixed, "space", d) for d in (1, 2, 3)]
    dlatent, dweight, dgamma, dbeta = kernel_step(
        final_body,
        [
            pltpu.HBM((local, cap, cells, chans), BF16),
            pltpu.HBM((taps, GSZ, outs_ch), F32),
            jax.ShapeDtypeStruct((1, chans), F32),
            jax.ShapeDtypeStruct((1, chans), F32),
        ],
        home + mixes + [keep, got1, got2],
        [
            VMEM((local * cap, HALF * NZ * NS, GSZ, cells), BF16),
            VMEM((local, cap, cells, chans), BF16),
            VMEM((taps, GSZ, outs_ch), F32),
            pltpu.SemaphoreType.DMA((local * cap + 1,)),
        ],
    )
    return (dlatent[None], dweight.transpose(1, 0, 2), dgamma.reshape(chans), dbeta.reshape(chans))


def fits_plan(sizes, latents, weight, upstream):
    return (
        sizes == [HALF, NZ, NS]
        and weight.shape[0] == GSZ
        and latents.shape[4] == GROUPS * GSZ
        and latents.shape[0] == 1
        and latents.shape[2] == CAP
        and upstream.shape[2] == 1
        and latents.shape[3] == LANES
    )


def body(latents, owner, gamma, beta, weight, upstream):
    args = (latents, owner, gamma, beta, weight, upstream)
    sizes = [lax.axis_size(a) for a in ("dp", "tm", "space")]
    if not fits_plan(sizes, latents, weight, upstream):
        return shards(*args)
    return channel_plan(*args)


def solution(mesh):
    return jax.shard_map(
        body,
        mesh=mesh,
        in_specs=(
            P("dp", "tm", "space", None, None),
            P("dp", None, None),
            P(),
            P(),
            P(("dp", "tm", "space"), None, None),
            P("dp", "tm", "space", None, None),
        ),
        out_specs=(
            P("dp", "tm", "space", None, None),
            P(("dp", "tm", "space"), None, None),
            P(),
            P(),
        ),
        check_vma=False,
    )
```

```python
import math

import jax
import jax.numpy as jnp
from jax import lax
from jax.experimental import pallas as pl
from jax.experimental.pallas import tpu as pltpu
from jax.sharding import PartitionSpec as P


GROUPS = 32
TH = 8
TW = 16


EPS = 1e-06


def shifted(value, axis, steps):
    count = lax.axis_size(axis)
    initial, last = (max(0, -steps), min(count, count - steps))
    return lax.ppermute(value, axis, [(source, source + steps) for source in range(initial, last)])


def tap_list():
    return [(kt, ky, kx) for kt in range(3) for ky in range(3) for kx in range(3)]


def conv_grads(hidden, grads, weight, rscale):
    frames, count, cells, chans = hidden.shape
    outs_ch = grads.shape[3]
    first_dev = lax.axis_index("tm") == 0
    cache = shifted(hidden, "tm", 1)
    repeat = jnp.concatenate([hidden[:1], hidden[:1]], axis=0)
    cache = jnp.where(first_dev, repeat, cache)
    extended = jnp.concatenate([cache, hidden], axis=0).reshape(frames + 2, count, TH, TW, chans)
    padded = jnp.pad(extended, ((0, 0), (0, 0), (1, 1), (1, 1), (0, 0)))
    rows = grads.reshape(frames * count * cells, outs_ch)
    span = lax.axis_size(("dp", "tm", "space")) * weight.shape[0]
    terms = []
    for kt, ky, kx in tap_list():
        tap = padded[kt : kt + frames, :, ky : ky + TH, kx : kx + TW].reshape(
            frames * count * cells, span
        )
        terms.append(
            lax.dot_general(tap, rows, (((0,), (0,)), ((), ())), preferred_element_type=jnp.float32)
        )
    dweight = lax.psum_scatter(
        jnp.stack(terms, axis=1) * rscale, ("dp", "tm", "space"), scatter_dimension=0, tiled=True
    )
    piece = lax.all_gather(weight, ("dp", "tm", "space"), axis=0, tiled=True)
    span = piece.shape[0]
    total = jnp.zeros((frames + 2, count, TH + 2, TW + 2, span), jnp.float32)
    for index, (kt, ky, kx) in enumerate(tap_list()):
        back = lax.dot_general(
            rows, piece[:, index, :], (((1,), (1,)), ((), ())), preferred_element_type=jnp.float32
        )
        total = total.at[kt : kt + frames, :, ky : ky + TH, kx : kx + TW].add(
            back.reshape(frames, count, TH, TW, span)
        )
    dextended = total[:, :, 1 : TH + 1, 1 : TW + 1].reshape(frames + 2, count, cells, span)
    carried = shifted(dextended[:2].astype(jnp.bfloat16), "tm", -1).astype(jnp.float32)
    own_part = dextended[2:]
    own_part = own_part.at[frames - 2 :].add(carried)
    own_part = own_part.at[0].add(jnp.where(first_dev, dextended[0] + dextended[1], 0.0))
    return (own_part, dweight)


def shards(latents, owner, gamma, beta, weight, upstream):
    blocks = latents[0]
    frames, cap, cells, chans = blocks.shape
    spaces = lax.axis_size("space")
    here = lax.axis_index("space")
    per_dev = upstream.shape[2]
    outs_ch = upstream.shape[4]
    tile_ids = owner[0, :, 0]
    tiles = tile_ids.shape[0]
    width = chans // GROUPS
    hot = (tile_ids[:, None] == jnp.arange(spaces, dtype=jnp.int32)[None, :]).astype(jnp.int32)
    rank = jnp.sum((jnp.cumsum(hot, axis=0) - hot) * hot, axis=1)
    slot = tile_ids * cap + rank
    holds = slot[None, :] == (here * cap + jnp.arange(cap, dtype=jnp.int32))[:, None]
    live = jnp.any(holds, axis=1).astype(jnp.float32)
    tile_of = jnp.sum(holds.astype(jnp.int32) * jnp.arange(tiles, dtype=jnp.int32)[None, :], axis=1)
    frames_all = frames * lax.axis_size("tm")
    count = float(frames_all * tiles * cells * width)
    rscale = 1.0 / math.sqrt(lax.axis_size("dp") * frames_all * tiles * cells)
    values = blocks.astype(jnp.float32).reshape(frames, cap, cells, GROUPS, width)
    live_mask = live[None, :, None, None, None]
    total = lax.psum(jnp.sum(values * live_mask, axis=(0, 1, 2, 4)), ("tm", "space"))
    mean = total / count
    centred = values - mean[:, None]
    spread = lax.psum(jnp.sum(centred * centred * live_mask, axis=(0, 1, 2, 4)), ("tm", "space"))
    var = spread / count
    inverse = lax.rsqrt(var + EPS)
    normed = (centred * inverse[:, None]).reshape(frames, cap, cells, chans)
    act = normed * gamma + beta
    sig = jax.nn.sigmoid(act)
    hidden = (act * sig).astype(jnp.bfloat16)
    ups = upstream[0].astype(jnp.float32).reshape(frames, per_dev, TH, 2, TW, 2, outs_ch)
    pooled = jnp.sum(ups, axis=(3, 5)).reshape(frames, per_dev, cells, outs_ch).astype(jnp.bfloat16)
    all_pooled = lax.all_gather(pooled, "space", axis=1, tiled=True)
    live_slot = live[None, :, None, None] > 0.5
    grads = jnp.where(live_slot, all_pooled[:, tile_of], jnp.zeros((), jnp.bfloat16))
    dhidden, dweight = conv_grads(hidden, grads, weight, rscale)
    dact = dhidden * (sig * (1.0 + act * (1.0 - sig))) * live[None, :, None, None]
    dgamma, dbeta = lax.psum(
        (jnp.sum(dact * normed, axis=(0, 1, 2)) * rscale, jnp.sum(dact, axis=(0, 1, 2)) * rscale),
        ("dp", "tm", "space"),
    )
    dnorm = (dact * gamma).reshape(frames, cap, cells, GROUPS, width)
    ngroup = normed.reshape(frames, cap, cells, GROUPS, width)
    first_m, second_m = lax.psum(
        (jnp.sum(dnorm, axis=(0, 1, 2, 4)), jnp.sum(dnorm * ngroup, axis=(0, 1, 2, 4))),
        ("tm", "space"),
    )
    dvalues = inverse[:, None] * (
        dnorm - (first_m / count)[:, None] - ngroup * (second_m / count)[:, None]
    )
    dfull = dvalues.reshape(frames, cap, cells, chans)
    resid = jnp.pad(grads.astype(jnp.float32), ((0, 0), (0, 0), (0, 0), (0, chans - outs_ch)))
    dlatent = ((dfull + resid) * live[None, :, None, None]).astype(jnp.bfloat16)
    return (dlatent[None], dweight, dgamma, dbeta)


LANES = 128
HALF = 2
NZ = 4
NS = 4
CAP = 2
GSZ = 16
FIRST_TAPS = 18
WIDE = HALF * GSZ

F32 = jnp.float32
BF16 = jnp.bfloat16
VMEM = pltpu.VMEM


def swap(value, axis, mask):
    count = lax.axis_size(axis)
    return lax.ppermute(value, axis, [(i, i ^ mask) for i in range(count)])


def kernel_step(body, outs, ins, scratch=(), entry=(), scalars=(), limit=24):
    held = [pltpu.with_memory_space_constraint(a, VMEM) for a in ins]
    small = [pltpu.with_memory_space_constraint(a, pltpu.SMEM) for a in scalars]
    return pl.pallas_call(
        body,
        out_shape=outs,
        in_specs=[pl.BlockSpec(memory_space=pltpu.SMEM)] * len(small)
        + [pl.BlockSpec(memory_space=pltpu.HBM)] * len(entry)
        + [pl.BlockSpec(memory_space=VMEM)] * len(held),
        out_specs=jax.tree.map(space_of, outs),
        scratch_shapes=list(scratch),
        compiler_params=pltpu.CompilerParams(vmem_limit_bytes=limit * 1024 * 1024),
    )(*small, *[pltpu.with_memory_space_constraint(a, pltpu.HBM) for a in entry], *held)


def space_of(out):
    return pl.BlockSpec(memory_space=getattr(out, "memory_space", VMEM))


def prep_body(up_hbm, lat_hbm, gamma_hbm, beta_hbm, own_hbm, *rest):
    (o0, o1, o2, o3, g_ref, gain, shift, spots) = rest[:8]
    buf, up_ref, lat_ref, gamma_ref, beta_ref, own_ref, sem = rest[8:]
    wanted = ((up_hbm, up_ref), (lat_hbm, lat_ref), (gamma_hbm, gamma_ref))
    wanted = wanted + ((beta_hbm, beta_ref), (own_hbm, own_ref))
    copies = [
        pltpu.make_async_copy(src, dst, sem.at[n]) for n, (src, dst) in enumerate(wanted)
    ]
    for copy in copies:
        copy.start()
    here = lax.axis_index("space")
    frames, cap, cells = lat_ref.shape[:3]
    fine = up_ref.shape[1]
    q = lax.broadcasted_iota(jnp.int32, (cells, fine), 0)
    p = lax.broadcasted_iota(jnp.int32, (cells, fine), 1)
    coarse = (p >> 6) * TW + ((p & (2 * TW - 1)) >> 1)
    mix = jnp.where(coarse == q, 1.0, 0.0).astype(BF16)
    slots = NZ * frames * cap * HALF
    copies[0].wait()
    for f in range(frames):
        pooled = jnp.dot(mix, up_ref[f], preferred_element_type=F32).astype(BF16)
        for o in range(pooled.shape[1] // LANES):
            part = pooled[:, o * LANES : (o + 1) * LANES]
            g_ref[f, o] = part
            rows = cells // GSZ
            base = slots + (f * 2 + o) * rows
            o1[base : base + rows] = part.reshape(rows, GSZ, LANES)
            o2[base : base + rows] = part.reshape(rows, GSZ, LANES)
    copies[1].wait()
    for f in range(frames):
        for c in range(cap):
            buf[...] = lat_ref[f, c].T.reshape(buf.shape)
            for d, out in enumerate((o0, o1, o2, o3)):
                for z in range(NZ):
                    for h in range(HALF):
                        at = ((z * frames + f) * cap + c) * HALF + h
                        out[at] = buf[h * NZ * NS + z * NS + (here ^ d)]
    copies[2].wait()
    copies[3].wait()
    slot = lax.axis_index("tm") * NS + here
    gain[...] = jnp.broadcast_to(own_channels(gamma_ref, slot), gain.shape)
    shift[...] = jnp.broadcast_to(own_channels(beta_ref, slot), shift.shape)
    copies[4].wait()
    for t, (who, rank) in enumerate(ranks(own_ref)):
        spots[2 * t] = who
        spots[2 * t + 1] = rank


def ranks(own_ref):
    out = []
    for t in range(own_ref.shape[0]):
        rank = jnp.int32(0)
        for before in range(t):
            rank = rank + jnp.where(own_ref[before] == own_ref[t], 1, 0)
        out.append((own_ref[t], rank))
    return out


def pick_body(spots, s0, s1, s2, s3, o0, o1, o2, o3):
    here, zed = lax.axis_index("space"), lax.axis_index("tm")
    frames = o0.shape[0]
    for t in range(o0.shape[1]):
        who, rank = spots[2 * t], spots[2 * t + 1]
        for d, src in enumerate((s0, s1, s2, s3)):

            @pl.when(who == (here ^ d))
            def _(src=src, t=t, rank=rank):
                for e, out in enumerate((o0, o1, o2, o3)):
                    for f in range(frames):
                        at = (((zed ^ e) * frames + f) * CAP + rank) * HALF
                        for h in range(HALF):
                            out[f, t, h] = src[at + h]


def join_body(a1, a3, out):
    out[0] = a1[...]
    out[1] = a3[...]


def by_group(rows, top, low):
    return jnp.where(rows < GSZ, top, low)


def own_channels(ref, slot):
    count = ref.shape[1]
    k = lax.broadcasted_iota(jnp.int32, (WIDE, count), 0)
    c = lax.broadcasted_iota(jnp.int32, (WIDE, count), 1)
    wanted = (k >> 4) * (count // HALF) + slot * GSZ + (k & (GSZ - 1))
    return jnp.sum(jnp.where(c == wanted, ref[...], 0.0), axis=1, keepdims=True)


def act_body(gain_ref, shift_ref, q0, q1, q2, q3, xh_ref, ds_ref, sh_ref, inv_ref):
    here, zed = lax.axis_index("space"), lax.axis_index("tm")
    local, tiles = q0.shape[:2]
    frames = xh_ref.shape[0]
    shape = (WIDE, LANES)
    rows = lax.broadcasted_iota(jnp.int32, shape, 0)
    lane = lax.broadcasted_iota(jnp.int32, shape, 1)
    count = float(frames * tiles * LANES * GSZ)
    acc = jnp.zeros(shape, F32)
    for e, q in enumerate((q0, q1, q2, q3)):
        for f in range(local):
            for t in range(tiles):
                x = q[f, here ^ t].astype(F32).reshape(shape)
                xh_ref[(zed ^ e) * local + f, t] = x
                acc = acc + x
    mean = by_group(rows, jnp.sum(acc[:GSZ]), jnp.sum(acc[GSZ:])) / count

    def spread_of(f, acc):
        for t in range(tiles):
            c = xh_ref[f, t] - mean
            acc = acc + c * c
        return acc

    acc = lax.fori_loop(0, frames, spread_of, jnp.zeros(shape, F32))
    var = by_group(rows, jnp.sum(acc[:GSZ]), jnp.sum(acc[GSZ:])) / count
    inv = lax.rsqrt(var + EPS)
    gain, shift = gain_ref[...], shift_ref[...]
    inv_ref[...] = inv
    col, row = lane & (TW - 1), lane >> 4

    def emit(f, carry):
        for t in range(tiles):
            normed = (xh_ref[f, t] - mean) * inv
            act = normed * gain + shift
            sig = jax.nn.sigmoid(act)
            hid = (act * sig).astype(BF16).astype(F32)
            xh_ref[f, t] = normed
            ds_ref[f, t] = sig * (1.0 + act * (1.0 - sig))
            left = jnp.where(col >= 1, pltpu.roll(hid, 1, 1), 0.0)
            right = jnp.where(col <= TW - 2, pltpu.roll(hid, LANES - 1, 1), 0.0)
            for kx, part in enumerate((left, hid, right)):
                up = jnp.where(row >= 1, pltpu.roll(part, TW, 1), 0.0)
                down = jnp.where(row <= TH - 2, pltpu.roll(part, LANES - TW, 1), 0.0)
                for ky, tap in enumerate((up, part, down)):
                    tap = tap.astype(BF16)
                    base = (ky * 3 + kx) * GSZ
                    for h in range(HALF):
                        sh_ref[f + 2, h, base : base + GSZ, t * LANES : (t + 1) * LANES] = tap[
                            h * GSZ : (h + 1) * GSZ
                        ]
        return carry

    lax.fori_loop(0, frames, emit, 0)
    sh_ref[0] = sh_ref[2]
    sh_ref[1] = sh_ref[2]


def place(gv, row, own, two, odd):
    zed = lax.axis_index("tm")
    local, cells = two.shape[0], two.shape[2]
    steps = cells // GSZ
    rows = slice(row, row + cells)
    for f in range(local):
        for o in range(2):
            lanes = slice(o * LANES, (o + 1) * LANES)
            if len(own.shape) == 3:
                at = own.shape[0] - (local * 2 - f * 2 - o) * steps
                gv[zed * local + f, rows, lanes] = own[at : at + steps].reshape(cells, LANES)
            else:
                gv[zed * local + f, rows, lanes] = own[f, o]
            gv[(zed ^ 2) * local + f, rows, lanes] = two[f, o]
            for e in (1, 3):
                gv[(zed ^ e) * local + f, rows, lanes] = odd[e // 2, f, o]
    frames = local * NZ
    for f in range(frames, frames + 2):
        gv[f, rows] = jnp.zeros((cells, gv.shape[2]), BF16)


def dot_nt(a, b):
    return lax.dot_general(a, b, (((1,), (1,)), ((), ())), preferred_element_type=F32)


def unshift(p, col, row):
    out = None
    for ky in range(3):
        part = [p[(ky * 3 + kx) * WIDE : (ky * 3 + kx + 1) * WIDE] for kx in range(3)]
        r = part[1]
        r = r + jnp.where(col <= TW - 2, pltpu.roll(part[0], LANES - 1, 1), 0.0)
        r = r + jnp.where(col >= 1, pltpu.roll(part[2], 1, 1), 0.0)
        if ky == 0:
            r = jnp.where(row <= TH - 2, pltpu.roll(r, LANES - TW, 1), 0.0)
        if ky == 2:
            r = jnp.where(row >= 1, pltpu.roll(r, TW, 1), 0.0)
        out = r if out is None else out + r
    return out


def hidden_grads(wv, gv, row, tiles, dh, res):
    shape = (WIDE, LANES)
    lane = lax.broadcasted_iota(jnp.int32, shape, 1)
    col, line = lane & (TW - 1), lane >> 4
    outs_ch = gv.shape[2]
    wide = 9 * WIDE
    frames = gv.shape[0] - 2
    step = 4 // tiles
    rows = slice(row, row + tiles * LANES)

    def grads_at(f, n=step):
        return gv[pl.ds(f, n), rows].reshape(n * tiles * LANES, outs_ch)

    def group(f, first):
        beside = jnp.concatenate([grads_at(f), grads_at(f + 1), grads_at(f + 2)], axis=1)
        total = dot_nt(wv[...].reshape(-1, 3 * outs_ch), beside)
        extra = None
        if first:
            now, then = grads_at(0, 1), grads_at(1, 1)
            late = wv[:9].reshape(wide, 3 * outs_ch)[:, outs_ch:]
            extra = dot_nt(late, jnp.concatenate([now, now], axis=1))
            extra = extra + dot_nt(late[:, outs_ch:], then)
        for n in range(step):
            for t in range(tiles):
                at = (n * tiles + t) * LANES
                p = total[:wide, at : at + LANES]
                if first and n == 0:
                    p = p + extra[:, t * LANES : (t + 1) * LANES]
                dh[f + n, t] = unshift(p, col, line)
                res[f + n, t] = total[wide : wide + GSZ, at : at + LANES]

    group(0, True)

    def later(n, carry):
        group(n * step, False)
        return carry

    lax.fori_loop(1, frames // step, later, 0)


def grad_near_body(wo, wp, g, a2, a13, r1, c2, c13, wv, gv, dh, res):
    zed, clip, here = lax.axis_index("tm"), lax.axis_index("dp"), lax.axis_index("space")
    outs_ch = wo.shape[2]
    for kt in range(3):
        lanes = slice((2 - kt) * outs_ch, (3 - kt) * outs_ch)
        for k in range(9):
            wv[k, clip, :, lanes] = wo[9 * kt + k]
            wv[k, 1 - clip, :, lanes] = wp[9 * kt + k]
    first = (zed * NS + here) * GSZ
    kk = lax.broadcasted_iota(jnp.int32, (GSZ, 3 * outs_ch), 0)
    oo = lax.broadcasted_iota(jnp.int32, (GSZ, 3 * outs_ch), 1)
    wv[9, 0] = jnp.where(oo == kk + first, 1.0, 0.0).astype(BF16)
    wv[9, 1] = jnp.zeros((GSZ, 3 * outs_ch), BF16)
    place(gv, 0, g, a2, a13)
    place(gv, LANES, r1, c2, c13)
    hidden_grads(wv, gv, 0, 2, dh, res)


def grad_far_body(wv, r2, y2, y13, gv, dh, res):
    place(gv, 0, r2, y2, y13)
    hidden_grads(wv, gv, 0, 1, dh, res)


def grad_last_body(wv, gv2, d0, d2, d13, dh01, res01, dh2, res2, xh, ds, gain_ref, inv_ref, *rest):
    (o0, o1, o2, o3, gv), (dh3, res3, dact) = rest[:5], rest[5:]
    here, zed = lax.axis_index("space"), lax.axis_index("tm")
    frames, tiles = xh.shape[:2]
    local = frames // NZ
    gv[:, :LANES] = gv2[...]
    place(gv, LANES, d0, d2, d13)
    hidden_grads(wv, gv, LANES, 1, dh3, res3)
    shape = (WIDE, LANES)
    rows = lax.broadcasted_iota(jnp.int32, shape, 0)
    lane = lax.broadcasted_iota(jnp.int32, shape, 1)
    parts = ((dh01, res01, 0), (dh01, res01, 1), (dh2, res2, 0), (dh3, res3, 0))

    def sums_of(f, sums):
        dg, db = sums
        for t, (dh, _, at) in enumerate(parts):
            da = dh[f, at] * ds[f, t]
            dact[f, t] = da
            dg = dg + da * xh[f, t]
            db = db + da
        return dg, db

    zero = jnp.zeros(shape, F32)
    dg, db = lax.fori_loop(0, frames, sums_of, (zero, zero))
    dg = jnp.sum(dg, axis=1, keepdims=True)
    db = jnp.sum(db, axis=1, keepdims=True)
    gain = gain_ref[...]
    inv = inv_ref[...]
    count = float(frames * tiles * LANES * GSZ)
    gb, gg = gain[:, :1] * db, gain[:, :1] * dg
    m1 = by_group(rows, jnp.sum(gb[:GSZ]), jnp.sum(gb[GSZ:])) / count
    m2 = by_group(rows, jnp.sum(gg[:GSZ]), jnp.sum(gg[GSZ:])) / count
    outs = (o0, o1, o2, o3)
    for e, out in enumerate(outs):
        for f in range(local):
            frame = (zed ^ e) * local + f
            for t, (_, res, at) in enumerate(parts):
                y = inv * (dact[frame, t] * gain - m1 - xh[frame, t] * m2)
                base = (f * tiles + (here ^ t)) * HALF
                out[base] = (y[:GSZ] + res[frame, at]).astype(BF16)
                out[base + 1] = y[GSZ:].astype(BF16)
    rscale = 1.0 / math.sqrt(lax.axis_size("dp") * frames * tiles * LANES)
    spot = lane == zed * WIDE + rows
    line = lax.broadcasted_iota(jnp.int32, (GSZ, LANES), 0)
    block = jnp.zeros((GSZ, LANES), F32)
    at = 0
    for value in (dg, db):
        value = jnp.sum(jnp.where(spot, value * rscale, 0.0), axis=0, keepdims=True)
        for _ in range(3):
            part = value.astype(BF16).astype(F32)
            block = jnp.where(line == at, part, block)
            value = value - part
            at += 1
    for out in outs:
        out[local * tiles * HALF] = block.astype(BF16)


def dweight_body(flip, sh_ref, near, far, *rest):
    outs, acc = rest[:-1], rest[-1]
    half = lax.axis_index("dp") ^ flip
    frames = near.shape[0] - 2
    pair = near.shape[1]
    acc[...] = jnp.zeros_like(acc)

    def frames_pair(n, carry):
        at = [2 * n, 2 * n + 1]
        taps = [sh_ref[pl.ds(f, 3), half].reshape(acc.shape[0], 2 * pair) for f in at]
        rows = [part[f] for f in at for part in (near, far)]
        acc[...] += jnp.dot(
            jnp.concatenate(taps, axis=1),
            jnp.concatenate(rows, axis=0),
            preferred_element_type=F32,
        )
        return carry

    lax.fori_loop(0, frames // 2, frames_pair, 0)
    rscale = 1.0 / math.sqrt(lax.axis_size("dp") * frames * 2 * pair)
    total = (acc[...] * rscale).reshape(-1, GSZ, acc.shape[1])
    start = 0
    for out in outs:
        out[...] = total[start : start + out.shape[0]]
        start += out.shape[0]


def expand_body(spots, p0, p1, p2, p3, o0, o1, o2, o3, sums):
    here, zed = lax.axis_index("space"), lax.axis_index("tm")
    tiles = spots.shape[0] // 2
    local = (p0.shape[0] - 1) // tiles // HALF
    parts, outs = (p0, p1, p2, p3), (o0, o1, o2, o3)
    for out in outs:
        out[...] = jnp.zeros_like(out)
    block = jnp.zeros((GSZ, LANES), F32)
    for part in parts:
        block = block + part[local * tiles * HALF].astype(F32)
    sums[0:1] = block[0:1] + block[1:2] + block[2:3]
    sums[1:2] = block[3:4] + block[4:5] + block[5:6]
    sums[2:8] = jnp.zeros((6, LANES), F32)
    for t in range(tiles):
        who, rank = spots[2 * t], spots[2 * t + 1]
        for d, out in enumerate(outs):

            @pl.when(who == (here ^ d))
            def _(out=out, t=t, rank=rank):
                for e, part in enumerate(parts):
                    for f in range(local):
                        at = (((zed ^ e) * local + f) * CAP + rank) * HALF
                        base = (f * tiles + t) * HALF
                        for h in range(HALF):
                            out[at + h] = part[base + h]


def mix_body(mine, peer, out):
    out[...] = mine[...] + peer[...]


def final_body(*refs):
    parts, sums, (keep, got1, got2) = refs[0:4], refs[4:8], refs[8:11]
    (out_hbm, dw_hbm, dg_hbm, db_hbm) = refs[11:15]
    (buf, out_ref, dw_ref, dg_ref, db_ref, sem) = refs[15:]
    here = lax.axis_index("space")
    frames, cap = out_ref.shape[:2]
    copies = []

    def send(src, dst):
        copies.append(pltpu.make_async_copy(src, dst, sem.at[len(copies)]))
        copies[-1].start()

    first = got1.shape[0]
    dw_ref[:first] = keep[:first] + got1[...]
    dw_ref[first:] = keep[first:] + got2[...]
    send(dw_ref, dw_hbm)
    chans = dg_ref.shape[1]
    lane = lax.broadcasted_iota(jnp.int32, (LANES, chans), 0)
    goal = lax.broadcasted_iota(jnp.int32, (LANES, chans), 1)
    source = ((goal >> 6) & 3) * WIDE + (goal >> 8) * GSZ + (goal & (GSZ - 1))
    sort = jnp.where(lane == source, 1.0, 0.0).astype(BF16)
    values = jnp.concatenate([part[...] for part in sums], axis=0)
    pieces = []
    for _ in range(3):
        pieces.append(values.astype(BF16))
        values = values - pieces[-1].astype(F32)
    moved = jnp.dot(jnp.concatenate(pieces, axis=0), sort, preferred_element_type=F32)
    count = values.shape[0]
    moved = moved[:count] + moved[count : 2 * count] + moved[2 * count :]
    owner = (lax.broadcasted_iota(jnp.int32, (8, chans), 1) >> 4) & 3
    total = jnp.zeros((8, chans), F32)
    for d in range(NS):
        total = jnp.where(owner == (here ^ d), moved[8 * d : 8 * d + 8], total)
    dg_ref[...] = total[0:1]
    db_ref[...] = total[1:2]
    send(dg_ref, dg_hbm)
    send(db_ref, db_hbm)
    for f in range(frames):
        for c in range(cap):
            spot = buf.at[f * cap + c]
            for d, part in enumerate(parts):
                for z in range(NZ):
                    for h in range(HALF):
                        at = ((z * frames + f) * cap + c) * HALF + h
                        spot[h * NZ * NS + z * NS + (here ^ d)] = part[at]
            out_ref[f, c] = spot[...].reshape(-1, LANES).T
            send(out_ref.at[f, c], out_hbm.at[f, c])
    for copy in copies:
        copy.wait()


def channel_plan(latents, owner, gamma, beta, weight, upstream):
    lat = latents[0]
    local, cap, cells, chans = lat.shape
    outs_ch = upstream.shape[4]
    tiles = owner.shape[1]
    frames = local * lax.axis_size("tm")
    taps = weight.shape[1]
    own = owner.reshape(tiles)
    slots = NZ * local * cap * HALF
    more = local * outs_ch // LANES * cells // GSZ
    own_w = weight.transpose(1, 0, 2)

    spread = [slots, slots + more, slots + more, slots]
    t0, t1, t2, t3, grads, gain, shift, spot_table = kernel_step(
        prep_body,
        [VMEM((count, GSZ, cells), BF16) for count in spread]
        + [
            VMEM((local, outs_ch // LANES, cells, LANES), BF16),
            VMEM((WIDE, LANES), F32),
            VMEM((WIDE, LANES), F32),
            pltpu.SMEM((2 * tiles,), jnp.int32),
        ],
        [],
        [
            VMEM((HALF * NZ * NS, GSZ, cells), BF16),
            VMEM((local, 4 * cells, outs_ch), BF16),
            VMEM(lat.shape, BF16),
            VMEM((1, chans), F32),
            VMEM((1, chans), F32),
            pltpu.SMEM((tiles,), jnp.int32),
            pltpu.SemaphoreType.DMA((5,)),
        ],
        entry=(
            upstream.reshape(local, 4 * cells, outs_ch),
            lat,
            gamma.reshape(1, chans),
            beta.reshape(1, chans),
            own,
        ),
    )
    along = [swap(grads, "tm", e) for e in (1, 2, 3)]
    r2, r3, r1 = (swap(v, "space", d) for v, d in ((t2, 2), (t3, 3), (t1, 1)))
    peer_w = swap(own_w, "dp", 1)
    d0 = swap(r2, "space", 1)
    picked = kernel_step(
        pick_body,
        [VMEM((local, tiles, HALF, GSZ, cells), BF16)] * NZ,
        [t0, r1, r2, r3],
        scalars=(spot_table,),
    )
    seen = [picked[0]] + [swap(picked[e], "tm", e) for e in (1, 2, 3)]
    a1, a2, a3 = along
    a13 = kernel_step(join_body, VMEM((2,) + grads.shape, BF16), [a1, a3])
    y2, c2 = swap(a2, "space", 2), swap(a2, "space", 1)
    y13, c13 = swap(a13, "space", 2), swap(a13, "space", 1)
    d2, d13 = swap(y2, "space", 1), swap(y13, "space", 1)
    normed, slope, shifts, inv = kernel_step(
        act_body,
        [
            VMEM((frames, tiles, WIDE, cells), F32),
            VMEM((frames, tiles, WIDE, cells), F32),
            VMEM((frames + 2, HALF, 9 * GSZ, tiles * cells), BF16),
            VMEM((WIDE, LANES), F32),
        ],
        [gain, shift] + seen,
    )

    def hidden_shapes(count):
        return [VMEM((frames, count, WIDE, cells), F32), VMEM((frames, count, GSZ, cells), F32)]

    taps_all, near, dh01, res01 = kernel_step(
        grad_near_body,
        [
            VMEM((10, HALF, GSZ, 3 * outs_ch), BF16),
            VMEM((frames + 2, 2 * cells, outs_ch), BF16),
        ]
        + hidden_shapes(2),
        [own_w, peer_w, grads, a2, a13, r1, c2, c13],
    )
    far2, dh2, res2 = kernel_step(
        grad_far_body,
        [VMEM((frames + 2, cells, outs_ch), BF16)] + hidden_shapes(1),
        [taps_all, r2, y2, y13],
    )
    shares = kernel_step(
        grad_last_body,
        [VMEM((local * tiles * HALF + 1, GSZ, cells), BF16)] * NZ
        + [VMEM((frames + 2, 2 * cells, outs_ch), BF16)],
        [taps_all, far2, d0, d2, d13, dh01, res01, dh2, res2, normed, slope, gain, inv],
        hidden_shapes(1) + [VMEM((frames, tiles, WIDE, cells), F32)],
    )
    far = shares[4]
    back = [shares[0]] + [swap(shares[e], "tm", e) for e in (1, 2, 3)]

    def dweight_half(flip, *parts):
        return kernel_step(
            lambda *refs: dweight_body(flip, *refs),
            [VMEM((part, GSZ, outs_ch), F32) for part in parts],
            [shifts, near, far],
            [VMEM((taps * GSZ, outs_ch), F32)],
        )

    send1, send2 = dweight_half(1, FIRST_TAPS, taps - FIRST_TAPS)
    got1, got2 = swap(send1, "dp", 1), swap(send2, "dp", 1)
    *spots, sums = kernel_step(
        expand_body,
        [VMEM((slots, GSZ, cells), BF16)] * NS + [VMEM((8, LANES), F32)],
        back,
        scalars=(spot_table,),
    )
    home = [spots[0]] + [swap(spots[d], "space", d) for d in (1, 2, 3)]
    (keep,) = dweight_half(0, taps)
    mixed = kernel_step(mix_body, VMEM((8, LANES), F32), [sums, swap(sums, "dp", 1)])
    mixes = [mixed] + [swap(mixed, "space", d) for d in (1, 2, 3)]
    dlatent, dweight, dgamma, dbeta = kernel_step(
        final_body,
        [
            pltpu.HBM((local, cap, cells, chans), BF16),
            pltpu.HBM((taps, GSZ, outs_ch), F32),
            pltpu.HBM((1, chans), F32),
            pltpu.HBM((1, chans), F32),
        ],
        home + mixes + [keep, got1, got2],
        [
            VMEM((local * cap, HALF * NZ * NS, GSZ, cells), BF16),
            VMEM((local, cap, cells, chans), BF16),
            VMEM((taps, GSZ, outs_ch), F32),
            VMEM((1, chans), F32),
            VMEM((1, chans), F32),
            pltpu.SemaphoreType.DMA((local * cap + 3,)),
        ],
    )
    return (dlatent[None], dweight.transpose(1, 0, 2), dgamma.reshape(chans), dbeta.reshape(chans))


def fits_plan(sizes, latents, weight, upstream):
    return (
        sizes == [HALF, NZ, NS]
        and weight.shape[0] == GSZ
        and latents.shape[4] == GROUPS * GSZ
        and latents.shape[0] == 1
        and latents.shape[2] == CAP
        and upstream.shape[2] == 1
        and latents.shape[3] == LANES
    )


def body(latents, owner, gamma, beta, weight, upstream):
    args = (latents, owner, gamma, beta, weight, upstream)
    sizes = [lax.axis_size(a) for a in ("dp", "tm", "space")]
    if not fits_plan(sizes, latents, weight, upstream):
        return shards(*args)
    return channel_plan(*args)


def solution(mesh):
    return jax.shard_map(
        body,
        mesh=mesh,
        in_specs=(
            P("dp", "tm", "space", None, None),
            P("dp", None, None),
            P(),
            P(),
            P(("dp", "tm", "space"), None, None),
            P("dp", "tm", "space", None, None),
        ),
        out_specs=(
            P("dp", "tm", "space", None, None),
            P(("dp", "tm", "space"), None, None),
            P(),
            P(),
        ),
        check_vma=False,
    )
```
